32 devices in a mesh: frame: 4 (over y, x), height: 2 (over core), width: 4 (over z).
Axes of the slice: x: 2, y: 2, z: 4, core: 2. Of those that a mesh axis runs over, the one named last changes fastest.
Arguments:
- tokens: bfloat16 [4, 16, 8, 16, 1536], P('frame', None, 'height', 'width'), may hold values from -6 to 6
- qkv_weight: bfloat16 [3, 768, 1536], P(None, ('frame', 'height')), may hold values from -0.15625 to 0.15625
- tile_mask: int32 [4, 4, 2, 4], P('frame'), may hold values 0 or 1
Outputs:
- attended: bfloat16 [4, 16, 8, 16, 768], P('frame', None, 'height', 'width')
The draws below stay inside these ranges and needn't reach their ends.
Inputs may be any that keep to these rules, and one draw needn't show every extreme that they name: `tile_mask`: selection flag of each tile.
All inputs are finite; a program needn't handle non-finite values. No bound on the sum of `tile_mask` on one device may be relied on, other than what follows from the above.
Results may differ from the reference program's by a relative error of at most 0.0082.
Values may be sent and summed in bfloat16 or wider, within the bound.
A program may use at most 64 MiB of HBM per device.

```python
import jax
import jax.numpy as jnp
from jax import lax

D = 1536
HEADS = 6
HEAD_DIM = 128
TILE = 4
FT = 4
HW = 768
CLIPS = 4
NF = 16
NH = 8
NW = 16


def plant(values, key, low, largest):
    index_at = [jax.random.randint(jax.random.fold_in(key, axis), (), 0, length) for axis, length in enumerate(values.shape)]
    main_axis = values.shape.index(max(values.shape))
    next_to = index_at[:main_axis] + [(index_at[main_axis] + 1) % values.shape[main_axis]] + index_at[main_axis + 1:]
    return values.at[tuple(index_at)].set(low).at[tuple(next_to)].set(largest)


def block_levels(rng, extent, pieces, smallest, largest):
    factor_of = 1.0
    for position, shards_of in pieces:
        draws = jax.random.uniform(jax.random.fold_in(jax.random.fold_in(rng, 6), position), (shards_of,), jnp.float32, smallest / len(pieces), largest / len(pieces))
        factor_of = factor_of * jnp.repeat(jnp.exp(draws), extent[position] // shards_of).reshape((-1,) + (1,) * (len(extent) - 1 - position))
    return factor_of


def normal_values(stream_key, dims, scale, limit, shards=(), kind=jnp.bfloat16):
    array = jax.random.normal(stream_key, dims, jnp.float32) * scale
    if len(shards) > 0:
        array = block_levels(stream_key, dims, shards, -0.22, 0.18) * array
    return jnp.clip(array, min=-limit, max=limit).astype(kind)


def setup_inputs(seed: int = 0) -> dict:
    key_list = jax.random.split(jax.random.key(seed), 4)
    return {
        "tokens": normal_values(key_list[0], (CLIPS, NF, NH, NW, D), 1.0, 6.0, ((0, 4), (2, 2), (3, 4))),
        "qkv_weight": normal_values(key_list[1], (3, HW, D), D ** -0.5, 0.15625, ((1, 8),)),
        "tile_mask": plant((jax.random.randint(key_list[2], (CLIPS, FT, NH // TILE, NW // TILE), 0, 4) < 3).astype(jnp.int32), jax.random.fold_in(key_list[2], 1), 0, 1),
    }


epsilon = 1e-06

def project_line(line_tokens, weight_wide):
    values_wide = line_tokens.astype(jnp.float32)
    normed = values_wide * lax.rsqrt(lax.optimization_barrier(jnp.mean(values_wide * values_wide, -1, keepdims=True)) + epsilon)
    normed = lax.optimization_barrier(normed.astype(jnp.bfloat16)).astype(jnp.float32)
    raw = jnp.einsum('td,shd->sth', normed, weight_wide)
    line_count = line_tokens.shape[0]
    head_view = raw[:2].reshape(2, line_count, HEADS, HEAD_DIM)
    scaled = head_view * lax.rsqrt(lax.optimization_barrier(jnp.mean(head_view * head_view, -1, keepdims=True)) + epsilon)
    scaled = scaled.reshape(2, line_count, HEADS * HEAD_DIM)
    return jnp.concatenate([scaled, raw[2:]], 0).astype(jnp.bfloat16)

def one_clip(clip_tokens, clip_mask, weight_wide):
    tiles_frame = NF // TILE
    tiles_height = NH // TILE
    tiles_width = NW // TILE
    cube = TILE * TILE * TILE
    lines = clip_tokens.reshape(NF * NH, NW, D)
    projected = lax.map(lambda line_tokens: project_line(line_tokens, weight_wide), lines)
    projected = jnp.transpose(projected, (1, 0, 2, 3)).reshape(3, NF, NH, NW, HW)
    tiled = projected.reshape(3, tiles_frame, TILE, tiles_height, TILE, tiles_width, TILE, HW)
    tiled = jnp.transpose(tiled, (0, 1, 3, 5, 2, 4, 6, 7)).reshape(3, tiles_frame, tiles_height, tiles_width, cube, HW)
    query_tiles = tiled[0]
    pad_spec = ((1, 1), (1, 1), (1, 1), (0, 0), (0, 0))
    key_tiles = jnp.pad(tiled[1], pad_spec)
    value_tiles = jnp.pad(tiled[2], pad_spec)
    mask_padded = jnp.pad(clip_mask, 1)
    zero_index = jnp.zeros((), jnp.int32)

    def window_block(source, frame_tile, height_tile):
        slab_tiles = lax.dynamic_slice(source, (frame_tile, height_tile, zero_index, zero_index, zero_index), (3, 3, tiles_width + 2, cube, HW))
        stacked = jnp.stack([slab_tiles[:, :, offset:offset + tiles_width] for offset in range(3)], 2)
        return jnp.moveaxis(stacked, 3, 0).reshape(tiles_width, 27 * cube, HW)

    def slab(slab_index):
        frame_tile = (slab_index // tiles_height).astype(jnp.int32)
        height_tile = (slab_index % tiles_height).astype(jnp.int32)
        key_block = window_block(key_tiles, frame_tile, height_tile)
        value_block = window_block(value_tiles, frame_tile, height_tile)
        mask_slab = lax.dynamic_slice(mask_padded, (frame_tile, height_tile, zero_index), (3, 3, tiles_width + 2))
        mask_stack = jnp.stack([mask_slab[:, :, offset:offset + tiles_width] for offset in range(3)], 2)
        mask_rows = jnp.moveaxis(mask_stack, 3, 0).reshape(tiles_width, 27)
        allowed = (mask_rows == 1) | (jnp.arange(27) == 13)[None, :]
        allowed = jnp.repeat(allowed, cube, axis=1)
        query_block = lax.dynamic_slice(query_tiles, (frame_tile, height_tile, zero_index, zero_index, zero_index), (1, 1, tiles_width, cube, HW))[0, 0]
        query_heads = query_block.astype(jnp.float32).reshape(tiles_width, cube, HEADS, HEAD_DIM)
        key_heads = key_block.astype(jnp.float32).reshape(tiles_width, 27 * cube, HEADS, HEAD_DIM)
        value_heads = value_block.astype(jnp.float32).reshape(tiles_width, 27 * cube, HEADS, HEAD_DIM)
        scores = jnp.einsum('cqhd,ckhd->chqk', query_heads, key_heads) * HEAD_DIM ** (-0.5)
        weight = jnp.where(allowed[:, None, None, :], jnp.exp(scores), jnp.float32(0.0))
        total = lax.optimization_barrier(jnp.sum(weight, -1))
        rounded = lax.optimization_barrier(weight.astype(jnp.bfloat16)).astype(jnp.float32)
        summed = jnp.einsum('chqk,ckhd->cqhd', rounded, value_heads)
        result = summed / jnp.moveaxis(total, 1, 2)[..., None]
        return result.reshape(tiles_width, cube, HW).astype(jnp.bfloat16)
    slabs = lax.map(slab, jnp.arange(tiles_frame * tiles_height, dtype=jnp.int32))
    attended = slabs.reshape(tiles_frame, tiles_height, tiles_width, TILE, TILE, TILE, HW)
    attended = jnp.transpose(attended, (0, 3, 1, 4, 2, 5, 6)).reshape(NF, NH, NW, HW)
    return attended

def reference(tokens, qkv_weight, tile_mask):
    weight_wide = qkv_weight.astype(jnp.float32)
    return lax.map(lambda pair: one_clip(pair[0], pair[1], weight_wide), (tokens, tile_mask))
```

```python
import functools
import math

import jax
import jax.numpy as jnp
from jax import lax
from jax.experimental import pallas as pl
from jax.experimental.pallas import tpu as pltpu
from jax.sharding import PartitionSpec as P

HEAD_DIM = 128
TILE = 4
VMEM_LIMIT = 54472 << 10
CUBE = TILE * TILE * TILE
MESH = pl.DeviceIdType.MESH

epsilon = 1e-06
QUERY, KEY, VALUE = 0, 1, 2


def kernel(
    n_h, n_w, x_ref, w_ref, tm_ref, o_ref,
    xs, xn, w_all, kbuf, vbuf, qbuf, mask,
    loc_sem, tok_s, tok_r, own_s, own_r, fwd_s, fwd_r, swap_s, swap_r, hgt_s, hgt_r, kvx_s, kvx_r,
):
    f, h, w = lax.axis_index("frame"), lax.axis_index("height"), lax.axis_index("width")
    f1 = f + 1 - 2 * (f % 2)
    f2 = f + 2 - 4 * ((f // 2) % 2)
    parity = f % 2
    side = w % 2
    rows = w_ref.shape[1]
    features = w_ref.shape[2]
    half = features // 2
    tokens = xn.shape[0] // 3
    frames = xs.shape[1]
    slots = kbuf.shape[0]
    heads = kbuf.shape[1] // 2
    group_rows = heads * HEAD_DIM
    local = n_h * rows // HEAD_DIM
    chunk = tokens // 2

    def place(owner_parity, group, row_parity, height):
        base = (owner_parity if group == 0 else 1 - owner_parity) * group_rows
        return pl.ds(pl.multiple_of(base + (row_parity * n_h + height) * rows, rows), rows)

    mine = place(parity, 0, parity, h)
    beside = place(parity, 0, 1 - parity, h)
    across = place(parity, 1, parity, h)
    corner = place(parity, 1, 1 - parity, h)

    def cols(s, p):
        at = p
        if s == QUERY:
            at = side if p == 0 else 1 - side
        return pl.ds(pl.multiple_of(at * half, half), half)

    def remote(src, dst, send, recv, target):
        return pltpu.make_async_remote_copy(
            src_ref=src, dst_ref=dst, send_sem=send, recv_sem=recv,
            device_id=target, device_id_type=MESH,
        )

    def to_frame(i):
        return ((f1, f2)[i], h, w)

    def own_copy(s, p, i):
        there = place(1 - parity, 0, parity, h) if i == 0 else across
        return remote(
            w_ref.at[s, :, cols(s, p)], w_all.at[s, there, cols(s, p)],
            own_s.at[s, p, i], own_r.at[s, p, i], to_frame(i),
        )

    def fwd_copy(s, i):
        if i == 1:
            src, there, at = beside, corner, cols(s, 0)
        else:
            src, there, at = across, place(1 - parity, 1, parity, h), cols(s, 1)
        return remote(w_all.at[s, src, at], w_all.at[s, there, at], fwd_s.at[s, i], fwd_r.at[s, i], to_frame(i))

    def swap_copy(i):
        part = w_all.at[QUERY, (beside, across)[i], cols(QUERY, i)]
        return remote(part, part, swap_s.at[i], swap_r.at[i], (f, h, w + 1 - 2 * side))

    def hgt_copy(s, piece, d):
        if piece == 0:
            src, dst = w_ref.at[s], w_all.at[s, mine]
        elif piece == 3:
            src = dst = w_all.at[s, corner]
        elif s != QUERY:
            src = dst = w_all.at[s, (beside, across)[piece - 1]]
        else:
            i = (piece - 1) % 3
            at = cols(s, i if piece < 3 else 1 - i)
            src = dst = w_all.at[s, (beside, across)[i], at]
        target = (f, lax.rem(h + d, n_h), w)
        return remote(src, dst, hgt_s.at[s, piece, d - 1], hgt_r.at[s, piece, d - 1], target)

    head_own = (parity * (2 * heads - local), local)
    head_beside = (local + parity * (heads - local), heads - local)
    head_across = (heads - parity * local, local)
    head_early = (parity * (heads - local), heads + local)
    head_late = ((1 - parity) * (heads + local), heads - local)

    kv_parts = (
        (head_early, 0, 2 * tokens),
        (head_early, 2 * tokens, tokens),
        (head_late, 0, 3 * tokens),
    )

    def kv_copy(which, part, up):
        buf = (kbuf, vbuf)[which]
        (first, count), start, length = kv_parts[part]
        slot = 1 if up or n_h == 2 else 2
        target = (f, h + 1 if up else h - 1, w)
        e = 0 if up else 1
        at = (pl.ds(first, count), pl.ds(start, length))
        return remote(
            buf.at[(0,) + at], buf.at[(slot,) + at], kvx_s.at[which, part, e], kvx_r.at[which, part, e], target
        )

    def tok_copy(e, c):
        target = (f, h, w + 1 if e == 0 else w - 1)
        at = pl.ds(c * (frames // 2), frames // 2)
        return remote(x_ref.at[0, at], xs.at[1 + e, at], tok_s.at[e, c], tok_r.at[e, c], target)

    local_x = pltpu.make_async_copy(x_ref.at[0], xs.at[0], loc_sem.at[0])
    local_w = [pltpu.make_async_copy(w_ref.at[s], w_all.at[s, mine], loc_sem.at[1 + s]) for s in range(3)]
    local_x.start()
    for s in (KEY, VALUE, QUERY):
        local_w[s].start()

    has_left, has_right = w > 0, w < n_w - 1
    has_below, has_above = h > 0, h < n_h - 1

    barrier = pltpu.get_barrier_semaphore()

    def greet(target):
        pl.semaphore_signal(barrier, inc=1, device_id=target, device_id_type=MESH)

    greet(to_frame(0))
    greet(to_frame(1))
    for d in range(1, n_h):
        greet((f, lax.rem(h + d, n_h), w))

    @pl.when(has_left)
    def _():
        greet((f, h, w - 1))

    @pl.when(has_right)
    def _():
        greet((f, h, w + 1))

    peers = n_h + 1 + has_left.astype(jnp.int32) + has_right.astype(jnp.int32)
    pl.semaphore_wait(barrier, peers)

    def send_own(s):
        own_copy(s, 0, 0).start()
        own_copy(s, 1, 1).start()
        if s != QUERY:
            own_copy(s, 1, 0).start()
            own_copy(s, 0, 1).start()

    def wait_own(s):
        own_copy(s, 0, 0).wait_recv()
        own_copy(s, 1, 1).wait_recv()
        fwd_copy(s, 0).start()
        fwd_copy(s, 1).start()
        if s == QUERY:
            swap_copy(0).start()
            swap_copy(1).start()
        else:
            own_copy(s, 1, 0).wait_recv()
            own_copy(s, 0, 1).wait_recv()
        relay(s, 1, 2)

    def relay(s, *pieces):
        for piece in pieces:
            for d in range(1, n_h):
                hgt_copy(s, piece, d).start()

    def take_fwd(s):
        fwd_copy(s, 0).wait_recv()
        fwd_copy(s, 1).wait_recv()
        relay(s, 3)

    def take_swap(i):
        swap_copy(i).wait_recv()
        relay(QUERY, 4 + i)

    def wait_hgt(s, *pieces):
        for piece in pieces:
            for d in range(1, n_h):
                hgt_copy(s, piece, d).wait_recv()

    for s in (KEY, VALUE, QUERY):
        send_own(s)
    for c in range(2):
        @pl.when(has_right)
        def _():
            tok_copy(0, c).start()

        @pl.when(has_left)
        def _():
            tok_copy(1, c).start()

    for s in (KEY, VALUE, QUERY):
        relay(s, 0)

    total_h, total_w = tm_ref.shape[2], tm_ref.shape[3]
    for b in range(slots):
        if b == 0:
            row_h = h
        elif n_h == 2:
            row_h = 1 - h
        else:
            row_h = h - 1 if b == 1 else h + 1

        def allow(c, first, count, start):
            shape = (tokens, count * CUBE)
            q_tile = lax.broadcasted_iota(jnp.int32, shape, 0) // CUBE
            k_tile = lax.broadcasted_iota(jnp.int32, shape, 1) // CUBE + first
            col_w = w + (0, -1, 1)[c]
            inside = ((row_h >= 0) & (row_h < total_h) & (col_w >= 0) & (col_w < total_w)).astype(jnp.int32)
            at_h = jnp.minimum(jnp.maximum(row_h, 0), total_h - 1)
            at_w = jnp.minimum(jnp.maximum(col_w, 0), total_w - 1)
            flags = jnp.zeros(shape, jnp.int32)
            for t in range(first, first + count):
                flag = tm_ref[0, t, at_h, at_w] * inside
                flags = jnp.where(k_tile == t, flag, flags)
            seen = flags == 1
            if b == 0 and c == 0:
                seen = seen | (q_tile == k_tile)
            allowed = jnp.where((jnp.abs(q_tile - k_tile) <= 1) & seen, jnp.float32(1.0), jnp.float32(0.0))
            mask[b, :, start : start + count * CUBE] = allowed.astype(jnp.bfloat16)

        allow(0, 0, tokens // CUBE, 0)
        for c in range(2):
            for e in range(2):
                allow(1 + e, c * (chunk // CUBE), chunk // CUBE, tokens + (2 * c + e) * chunk)

    step = 64

    def normalise(c, frame, start, count):
        for t in range(count // step):
            each = step // (TILE * TILE)
            block = xs[c, frame + t * each : frame + (t + 1) * each].astype(jnp.float32).reshape(step, features)
            scale = lax.rsqrt(jnp.mean(block * block, -1, keepdims=True) + epsilon)
            xn[start + t * step : start + (t + 1) * step, :] = (block * scale).astype(jnp.bfloat16)

    def take_tokens(c):
        for e, here in ((0, has_left), (1, has_right)):
            start = tokens + (2 * c + e) * chunk

            @pl.when(here)
            def _():
                tok_copy(e, c).wait_recv()
                normalise(1 + e, c * (frames // 2), start, chunk)

            @pl.when(jnp.logical_not(here))
            def _():
                xn[start : start + chunk, :] = jnp.zeros((chunk, features), jnp.bfloat16)

    def head_norm(raw):
        return (raw * lax.rsqrt(jnp.mean(raw * raw, -1, keepdims=True) + epsilon)).astype(jnp.bfloat16)

    contract_last = (((1,), (1,)), ((), ()))

    def project(s, some, start, length):
        first, count = some
        place_rows = pl.ds(pl.multiple_of(first * HEAD_DIM, HEAD_DIM), count * HEAD_DIM)
        raw = lax.dot_general(
            xn[start : start + length, :], w_all[s, place_rows], contract_last, preferred_element_type=jnp.float32
        )
        for j in range(count):
            part = raw[:, j * HEAD_DIM : (j + 1) * HEAD_DIM]
            if s == QUERY:
                qbuf[first + j] = head_norm(part)
            elif s == KEY:
                kbuf[0, first + j, start : start + length, :] = head_norm(part)
            else:
                vbuf[0, first + j, start : start + length, :] = part.astype(jnp.bfloat16)

    def send_kv(which, part):
        @pl.when(has_above)
        def _():
            kv_copy(which, part, True).start()

        @pl.when(has_below)
        def _():
            kv_copy(which, part, False).start()

    def wait_kv(*parts):
        for part in parts:
            for which in range(2):
                @pl.when(has_below)
                def _():
                    kv_copy(which, part, True).wait_recv()

                @pl.when(has_above)
                def _():
                    kv_copy(which, part, False).wait_recv()

    factor = HEAD_DIM ** (-0.5) * math.log2(math.e)
    ones = jnp.ones((3 * tokens, HEAD_DIM), jnp.bfloat16)
    pair = f // 2

    def attend(some):
        first, count = some

        def body(i, carry):
            j = first + i
            q = qbuf[j]
            total = jnp.zeros((tokens, 2 * HEAD_DIM), jnp.float32)
            for b in range(slots):
                scores = lax.dot_general(q, kbuf[b, j], contract_last, preferred_element_type=jnp.float32)
                weight = jnp.exp2(scores * factor).astype(jnp.bfloat16) * mask[b]
                wide = jnp.concatenate([vbuf[b, j], ones], 1)
                total = total + jnp.dot(weight, wide, preferred_element_type=jnp.float32)
            result = (total[:, :HEAD_DIM] / total[:, HEAD_DIM:]).astype(o_ref.dtype)
            upper = (j >= heads).astype(jnp.int32)
            group = lax.rem(pair + parity + upper, 2)
            at = (group * heads + j - upper * heads) * HEAD_DIM
            o_ref[:, pl.ds(pl.multiple_of(at, HEAD_DIM), HEAD_DIM)] = result
            return carry

        lax.fori_loop(0, count, body, 0)

    if n_h > 2:
        for edge, slot in ((h == 0, 1), (h == n_h - 1, 2)):
            @pl.when(edge)
            def _():
                kbuf[slot] = jnp.zeros(kbuf.shape[1:], jnp.bfloat16)
                vbuf[slot] = jnp.zeros(vbuf.shape[1:], jnp.bfloat16)

    local_x.wait()
    normalise(0, 0, 0, tokens)
    wait_own(KEY)
    take_tokens(0)
    local_w[KEY].wait()
    wait_hgt(KEY, 0, 1, 2)
    project(KEY, head_early, 0, 2 * tokens)
    send_kv(0, 0)
    wait_own(VALUE)
    local_w[VALUE].wait()
    wait_hgt(VALUE, 0, 1, 2)
    project(VALUE, head_early, 0, 2 * tokens)
    send_kv(1, 0)
    local_w[QUERY].wait()
    wait_hgt(QUERY, 0)
    project(QUERY, head_own, 0, tokens)
    wait_own(QUERY)
    take_tokens(1)
    project(KEY, head_early, 2 * tokens, tokens)
    send_kv(0, 1)
    project(VALUE, head_early, 2 * tokens, tokens)
    send_kv(1, 1)
    take_fwd(KEY)
    wait_kv(0, 1)
    attend(head_own)
    wait_hgt(KEY, 3)
    project(KEY, head_late, 0, 3 * tokens)
    send_kv(0, 2)
    take_swap(0)
    take_fwd(VALUE)
    wait_hgt(QUERY, 1, 4)
    project(QUERY, head_beside, 0, tokens)
    wait_hgt(VALUE, 3)
    project(VALUE, head_late, 0, 3 * tokens)
    send_kv(1, 2)
    attend(head_beside)
    take_swap(1)
    take_fwd(QUERY)
    wait_hgt(QUERY, 2, 5)
    project(QUERY, head_across, 0, tokens)
    attend(head_across)
    wait_kv(2)
    wait_hgt(QUERY, 3)
    project(QUERY, head_late, 0, tokens)
    attend(head_late)

    for s in range(3):
        for i in range(2):
            own_copy(s, i, i).wait_send()
            fwd_copy(s, i).wait_send()
            if s != QUERY:
                own_copy(s, 1 - i, i).wait_send()
        for piece in range(6 if s == QUERY else 4):
            for d in range(1, n_h):
                hgt_copy(s, piece, d).wait_send()
    for i in range(2):
        swap_copy(i).wait_send()

    for c in range(2):
        @pl.when(has_right)
        def _():
            tok_copy(0, c).wait_send()

        @pl.when(has_left)
        def _():
            tok_copy(1, c).wait_send()

    for part in range(3):
        for which in range(2):
            @pl.when(has_above)
            def _():
                kv_copy(which, part, True).wait_send()

            @pl.when(has_below)
            def _():
                kv_copy(which, part, False).wait_send()


def per_device(n_f, n_h, n_w, tokens, qkv_weight, tile_mask):
    clips, frames, rows, columns, features = tokens.shape
    count = frames * rows * columns
    width = qkv_weight.shape[1] * n_f * n_h
    if n_f != 4 or n_h < 2 or n_w % 2 or clips != 1 or rows != TILE or columns != TILE:
        raise ValueError("unsupported placement")
    heads = width // HEAD_DIM
    slots = 2 if n_h == 2 else 3
    dma = pltpu.SemaphoreType.DMA
    out = pl.pallas_call(
        functools.partial(kernel, n_h, n_w),
        out_shape=jax.ShapeDtypeStruct((count, width), jnp.bfloat16),
        in_specs=[
            pl.BlockSpec(memory_space=pl.ANY),
            pl.BlockSpec(memory_space=pl.ANY),
            pl.BlockSpec(memory_space=pltpu.SMEM),
        ],
        out_specs=pl.BlockSpec(memory_space=pltpu.VMEM),
        scratch_shapes=[
            pltpu.VMEM((3, frames, rows, columns, features), jnp.bfloat16),
            pltpu.VMEM((3 * count, features), jnp.bfloat16),
            pltpu.VMEM((3, width, features), jnp.bfloat16),
            pltpu.VMEM((slots, heads, 3 * count, HEAD_DIM), jnp.bfloat16),
            pltpu.VMEM((slots, heads, 3 * count, HEAD_DIM), jnp.bfloat16),
            pltpu.VMEM((heads, count, HEAD_DIM), jnp.bfloat16),
            pltpu.VMEM((slots, count, 3 * count), jnp.bfloat16),
            dma((4,)), dma((2, 2)), dma((2, 2)), dma((3, 2, 2)), dma((3, 2, 2)), dma((3, 2)), dma((3, 2)),
            dma((2,)), dma((2,)), dma((3, 6, n_h - 1)), dma((3, 6, n_h - 1)), dma((2, 3, 2)), dma((2, 3, 2)),
        ],
        compiler_params=pltpu.CompilerParams(
            collective_id=0, has_side_effects=True, vmem_limit_bytes=VMEM_LIMIT
        ),
    )(tokens, qkv_weight, tile_mask)
    return out.reshape(clips, frames, rows, columns, width)


def solution(mesh):
    in_specs = (
        P("frame", None, "height", "width", None),
        P(None, ("frame", "height"), None),
        P("frame", None, None, None),
    )
    out_specs = P("frame", None, "height", "width", None)
    body = functools.partial(
        per_device, mesh.shape["frame"], mesh.shape["height"], mesh.shape["width"]
    )
    return jax.shard_map(body, mesh=mesh, in_specs=in_specs, out_specs=out_specs, check_vma=False)
```

```python
import functools
import math

import jax
import jax.numpy as jnp
from jax import lax
from jax.experimental import pallas as pl
from jax.experimental.pallas import tpu as pltpu
from jax.sharding import PartitionSpec as P

HEAD_DIM = 128
TILE = 4
VMEM_LIMIT = 54472 << 10
CUBE = TILE * TILE * TILE
MESH = pl.DeviceIdType.MESH

epsilon = 1e-06
QUERY, KEY, VALUE = 0, 1, 2


def kernel(
    n_h, n_w, x_ref, w_ref, tm_ref, o_ref,
    xs, xn, w_all, kbuf, vbuf, qbuf, mask,
    loc_sem, tok_s, tok_r, own_s, own_r, fwd_s, fwd_r, swap_s, swap_r, hgt_s, hgt_r, kvx_s, kvx_r,
):
    f, h, w = lax.axis_index("frame"), lax.axis_index("height"), lax.axis_index("width")
    f1 = f + 1 - 2 * (f % 2)
    f2 = f + 2 - 4 * ((f // 2) % 2)
    parity = f % 2
    side = w % 2
    rows = w_ref.shape[1]
    features = w_ref.shape[2]
    half = features // 2
    tokens = xn.shape[0] // 3
    span = 3 * tokens
    slots = kbuf.shape[1] // span
    frames = xs.shape[1]
    heads = kbuf.shape[0] // 2
    group_rows = heads * HEAD_DIM
    local = n_h * rows // HEAD_DIM
    chunk = tokens // 2

    def place(owner_parity, group, row_parity, height):
        base = (owner_parity if group == 0 else 1 - owner_parity) * group_rows
        return pl.ds(pl.multiple_of(base + (row_parity * n_h + height) * rows, rows), rows)

    mine = place(parity, 0, parity, h)
    beside = place(parity, 0, 1 - parity, h)
    across = place(parity, 1, parity, h)
    corner = place(parity, 1, 1 - parity, h)

    def cols(s, p):
        at = p
        if s == QUERY:
            at = side if p == 0 else 1 - side
        return pl.ds(pl.multiple_of(at * half, half), half)

    def remote(src, dst, send, recv, target):
        return pltpu.make_async_remote_copy(
            src_ref=src, dst_ref=dst, send_sem=send, recv_sem=recv,
            device_id=target, device_id_type=MESH,
        )

    def to_frame(i):
        return ((f1, f2)[i], h, w)

    def own_copy(s, p, i):
        there = place(1 - parity, 0, parity, h) if i == 0 else across
        return remote(
            w_ref.at[s, :, cols(s, p)], w_all.at[s, there, cols(s, p)],
            own_s.at[s, p, i], own_r.at[s, p, i], to_frame(i),
        )

    def fwd_copy(s, i):
        if i == 1:
            src, there, at = beside, corner, cols(s, 0)
        else:
            src, there, at = across, place(1 - parity, 1, parity, h), cols(s, 1)
        return remote(w_all.at[s, src, at], w_all.at[s, there, at], fwd_s.at[s, i], fwd_r.at[s, i], to_frame(i))

    def swap_copy(i):
        part = w_all.at[QUERY, (beside, across)[i], cols(QUERY, i)]
        return remote(part, part, swap_s.at[i], swap_r.at[i], (f, h, w + 1 - 2 * side))

    def hgt_copy(s, piece, d):
        if piece == 0:
            src, dst = w_ref.at[s], w_all.at[s, mine]
        elif piece == 3:
            src = dst = w_all.at[s, corner]
        elif s != QUERY:
            src = dst = w_all.at[s, (beside, across)[piece - 1]]
        else:
            i = (piece - 1) % 3
            at = cols(s, i if piece < 3 else 1 - i)
            src = dst = w_all.at[s, (beside, across)[i], at]
        target = (f, lax.rem(h + d, n_h), w)
        return remote(src, dst, hgt_s.at[s, piece, d - 1], hgt_r.at[s, piece, d - 1], target)

    head_own = (parity * (2 * heads - local), local)
    head_beside = (local + parity * (heads - local), heads - local)
    head_other = ((1 - parity) * heads, heads)
    head_early = (parity * (heads - local), heads + local)
    head_late = ((1 - parity) * (heads + local), heads - local)

    kv_parts = (
        (head_early, 0, 2 * tokens),
        (head_early, 2 * tokens, tokens),
        (head_late, 0, 3 * tokens),
    )

    def kv_copy(which, part, up):
        buf = (kbuf, vbuf)[which]
        (first, count), start, length = kv_parts[part]
        slot = 1 if up or n_h == 2 else 2
        target = (f, h + 1 if up else h - 1, w)
        e = 0 if up else 1
        some = pl.ds(first, count)
        src = buf.at[some, pl.ds(start, length)]
        dst = buf.at[some, pl.ds(slot * span + start, length)]
        return remote(src, dst, kvx_s.at[which, part, e], kvx_r.at[which, part, e], target)

    def tok_copy(e, c):
        target = (f, h, w + 1 if e == 0 else w - 1)
        at = pl.ds(c * (frames // 2), frames // 2)
        return remote(x_ref.at[0, at], xs.at[1 + e, at], tok_s.at[e, c], tok_r.at[e, c], target)

    local_x = pltpu.make_async_copy(x_ref.at[0], xs.at[0], loc_sem.at[0])
    local_w = [pltpu.make_async_copy(w_ref.at[s], w_all.at[s, mine], loc_sem.at[1 + s]) for s in range(3)]
    local_x.start()
    for s in (KEY, VALUE, QUERY):
        local_w[s].start()

    has_left, has_right = w > 0, w < n_w - 1
    has_below, has_above = h > 0, h < n_h - 1

    barrier = pltpu.get_barrier_semaphore()

    def greet(target):
        pl.semaphore_signal(barrier, inc=1, device_id=target, device_id_type=MESH)

    greet(to_frame(0))
    greet(to_frame(1))
    for d in range(1, n_h):
        greet((f, lax.rem(h + d, n_h), w))

    @pl.when(has_left)
    def _():
        greet((f, h, w - 1))

    @pl.when(has_right)
    def _():
        greet((f, h, w + 1))

    peers = n_h + 1 + has_left.astype(jnp.int32) + has_right.astype(jnp.int32)
    pl.semaphore_wait(barrier, peers)

    def send_own(s):
        own_copy(s, 0, 0).start()
        own_copy(s, 1, 1).start()
        if s != QUERY:
            own_copy(s, 1, 0).start()
            own_copy(s, 0, 1).start()

    def wait_own(s):
        own_copy(s, 0, 0).wait_recv()
        own_copy(s, 1, 1).wait_recv()
        fwd_copy(s, 0).start()
        fwd_copy(s, 1).start()
        if s == QUERY:
            swap_copy(0).start()
            swap_copy(1).start()
        else:
            own_copy(s, 1, 0).wait_recv()
            own_copy(s, 0, 1).wait_recv()
        relay(s, 1, 2)

    def relay(s, *pieces):
        for piece in pieces:
            for d in range(1, n_h):
                hgt_copy(s, piece, d).start()

    def take_fwd(s):
        fwd_copy(s, 0).wait_recv()
        fwd_copy(s, 1).wait_recv()
        relay(s, 3)

    def take_swap(i):
        swap_copy(i).wait_recv()
        relay(QUERY, 4 + i)

    def wait_hgt(s, *pieces):
        for piece in pieces:
            for d in range(1, n_h):
                hgt_copy(s, piece, d).wait_recv()

    for s in (KEY, VALUE, QUERY):
        send_own(s)
    for c in range(2):
        @pl.when(has_right)
        def _():
            tok_copy(0, c).start()

        @pl.when(has_left)
        def _():
            tok_copy(1, c).start()

    for s in (KEY, VALUE, QUERY):
        relay(s, 0)

    total_h, total_w = tm_ref.shape[2], tm_ref.shape[3]
    for b in range(slots):
        if b == 0:
            row_h = h
        elif n_h == 2:
            row_h = 1 - h
        else:
            row_h = h - 1 if b == 1 else h + 1

        def allow(c, first, count, start):
            shape = (tokens, count * CUBE)
            q_tile = lax.broadcasted_iota(jnp.int32, shape, 0) // CUBE
            k_tile = lax.broadcasted_iota(jnp.int32, shape, 1) // CUBE + first
            col_w = w + (0, -1, 1)[c]
            inside = ((row_h >= 0) & (row_h < total_h) & (col_w >= 0) & (col_w < total_w)).astype(jnp.int32)
            at_h = jnp.minimum(jnp.maximum(row_h, 0), total_h - 1)
            at_w = jnp.minimum(jnp.maximum(col_w, 0), total_w - 1)
            flags = jnp.zeros(shape, jnp.int32)
            for t in range(first, first + count):
                flag = tm_ref[0, t, at_h, at_w] * inside
                flags = jnp.where(k_tile == t, flag, flags)
            seen = flags == 1
            if b == 0 and c == 0:
                seen = seen | (q_tile == k_tile)
            allowed = jnp.where((jnp.abs(q_tile - k_tile) <= 1) & seen, jnp.float32(1.0), jnp.float32(0.0))
            start = b * span + start
            mask[:, start : start + count * CUBE] = allowed.astype(jnp.bfloat16)

        allow(0, 0, tokens // CUBE, 0)
        for c in range(2):
            for e in range(2):
                allow(1 + e, c * (chunk // CUBE), chunk // CUBE, tokens + (2 * c + e) * chunk)

    step = 64

    def normalise(c, frame, start, count):
        for t in range(count // step):
            each = step // (TILE * TILE)
            block = xs[c, frame + t * each : frame + (t + 1) * each].astype(jnp.float32).reshape(step, features)
            scale = lax.rsqrt(jnp.mean(block * block, -1, keepdims=True) + epsilon)
            xn[start + t * step : start + (t + 1) * step, :] = (block * scale).astype(jnp.bfloat16)

    def take_tokens(c):
        for e, here in ((0, has_left), (1, has_right)):
            start = tokens + (2 * c + e) * chunk

            @pl.when(here)
            def _():
                tok_copy(e, c).wait_recv()
                normalise(1 + e, c * (frames // 2), start, chunk)

            @pl.when(jnp.logical_not(here))
            def _():
                xn[start : start + chunk, :] = jnp.zeros((chunk, features), jnp.bfloat16)

    def head_norm(raw):
        return (raw * lax.rsqrt(jnp.mean(raw * raw, -1, keepdims=True) + epsilon)).astype(jnp.bfloat16)

    contract_last = (((1,), (1,)), ((), ()))

    def project(s, some, start, length):
        first, count = some
        place_rows = pl.ds(pl.multiple_of(first * HEAD_DIM, HEAD_DIM), count * HEAD_DIM)
        raw = lax.dot_general(
            xn[start : start + length, :], w_all[s, place_rows], contract_last, preferred_element_type=jnp.float32
        )
        for j in range(count):
            part = raw[:, j * HEAD_DIM : (j + 1) * HEAD_DIM]
            if s == QUERY:
                qbuf[first + j] = head_norm(part)
            elif s == KEY:
                kbuf[first + j, start : start + length, :] = head_norm(part)
            else:
                vbuf[first + j, start : start + length, :] = part.astype(jnp.bfloat16)

    def send_kv(which, part):
        @pl.when(has_above)
        def _():
            kv_copy(which, part, True).start()

        @pl.when(has_below)
        def _():
            kv_copy(which, part, False).start()

    def wait_kv(*parts):
        for part in parts:
            for which in range(2):
                @pl.when(has_below)
                def _():
                    kv_copy(which, part, True).wait_recv()

                @pl.when(has_above)
                def _():
                    kv_copy(which, part, False).wait_recv()

    factor = HEAD_DIM ** (-0.5) * math.log2(math.e)
    ones = jnp.ones((slots * span, HEAD_DIM), jnp.bfloat16)
    pair = f // 2

    def attend(some):
        first, count = some

        for i in range(count):
            j = first + i
            scores = lax.dot_general(qbuf[j], kbuf[j], contract_last, preferred_element_type=jnp.float32)
            weight = jnp.exp2(scores * factor).astype(jnp.bfloat16) * mask[...]
            wide = jnp.concatenate([vbuf[j], ones], 1)
            total = jnp.dot(weight, wide, preferred_element_type=jnp.float32)
            result = (total[:, :HEAD_DIM] / total[:, HEAD_DIM:]).astype(o_ref.dtype)
            upper = (j >= heads).astype(jnp.int32)
            group = lax.rem(pair + parity + upper, 2)
            at = (group * heads + j - upper * heads) * HEAD_DIM
            o_ref[:, pl.ds(pl.multiple_of(at, HEAD_DIM), HEAD_DIM)] = result

    if n_h > 2:
        for edge, slot in ((h == 0, 1), (h == n_h - 1, 2)):
            @pl.when(edge)
            def _():
                at = slice(slot * span, (slot + 1) * span)
                kbuf[:, at] = jnp.zeros((2 * heads, span, HEAD_DIM), jnp.bfloat16)
                vbuf[:, at] = jnp.zeros((2 * heads, span, HEAD_DIM), jnp.bfloat16)

    local_x.wait()
    normalise(0, 0, 0, tokens)
    wait_own(KEY)
    take_tokens(0)
    local_w[KEY].wait()
    wait_hgt(KEY, 0, 1, 2)
    project(KEY, head_early, 0, 2 * tokens)
    send_kv(0, 0)
    wait_own(VALUE)
    local_w[VALUE].wait()
    wait_hgt(VALUE, 0, 1, 2)
    project(VALUE, head_early, 0, 2 * tokens)
    send_kv(1, 0)
    local_w[QUERY].wait()
    wait_hgt(QUERY, 0)
    project(QUERY, head_own, 0, tokens)
    wait_own(QUERY)
    take_tokens(1)
    project(KEY, head_early, 2 * tokens, tokens)
    send_kv(0, 1)
    take_fwd(KEY)
    project(VALUE, head_early, 2 * tokens, tokens)
    send_kv(1, 1)
    wait_hgt(KEY, 3)
    project(KEY, head_late, 0, 3 * tokens)
    send_kv(0, 2)
    take_swap(0)
    take_fwd(VALUE)
    wait_kv(0, 1)
    attend(head_own)
    wait_hgt(VALUE, 3)
    project(VALUE, head_late, 0, 3 * tokens)
    send_kv(1, 2)
    wait_hgt(QUERY, 1, 4)
    project(QUERY, head_beside, 0, tokens)
    take_swap(1)
    attend((head_beside[0], 1))
    take_fwd(QUERY)
    attend((head_beside[0] + 1, head_beside[1] - 1))
    wait_hgt(QUERY, 2, 5, 3)
    project(QUERY, head_other, 0, tokens)
    wait_kv(2)
    attend(head_other)

    for s in range(3):
        for i in range(2):
            own_copy(s, i, i).wait_send()
            fwd_copy(s, i).wait_send()
            if s != QUERY:
                own_copy(s, 1 - i, i).wait_send()
        for piece in range(6 if s == QUERY else 4):
            for d in range(1, n_h):
                hgt_copy(s, piece, d).wait_send()
    for i in range(2):
        swap_copy(i).wait_send()

    for c in range(2):
        @pl.when(has_right)
        def _():
            tok_copy(0, c).wait_send()

        @pl.when(has_left)
        def _():
            tok_copy(1, c).wait_send()

    for part in range(3):
        for which in range(2):
            @pl.when(has_above)
            def _():
                kv_copy(which, part, True).wait_send()

            @pl.when(has_below)
            def _():
                kv_copy(which, part, False).wait_send()


def per_device(n_f, n_h, n_w, tokens, qkv_weight, tile_mask):
    clips, frames, rows, columns, features = tokens.shape
    count = frames * rows * columns
    width = qkv_weight.shape[1] * n_f * n_h
    if n_f != 4 or n_h < 2 or n_w % 2 or clips != 1 or rows != TILE or columns != TILE:
        raise ValueError("unsupported placement")
    heads = width // HEAD_DIM
    slots = 2 if n_h == 2 else 3
    dma = pltpu.SemaphoreType.DMA
    out = pl.pallas_call(
        functools.partial(kernel, n_h, n_w),
        out_shape=jax.ShapeDtypeStruct((count, width), jnp.bfloat16),
        in_specs=[
            pl.BlockSpec(memory_space=pltpu.HBM),
            pl.BlockSpec(memory_space=pltpu.HBM),
            pl.BlockSpec(memory_space=pltpu.SMEM),
        ],
        out_specs=pl.BlockSpec(memory_space=pltpu.VMEM),
        scratch_shapes=[
            pltpu.VMEM((3, frames, rows, columns, features), jnp.bfloat16),
            pltpu.VMEM((3 * count, features), jnp.bfloat16),
            pltpu.VMEM((3, width, features), jnp.bfloat16),
            pltpu.VMEM((heads, slots * 3 * count, HEAD_DIM), jnp.bfloat16),
            pltpu.VMEM((heads, slots * 3 * count, HEAD_DIM), jnp.bfloat16),
            pltpu.VMEM((heads, count, HEAD_DIM), jnp.bfloat16),
            pltpu.VMEM((count, slots * 3 * count), jnp.bfloat16),
            dma((4,)), dma((2, 2)), dma((2, 2)), dma((3, 2, 2)), dma((3, 2, 2)), dma((3, 2)), dma((3, 2)),
            dma((2,)), dma((2,)), dma((3, 6, n_h - 1)), dma((3, 6, n_h - 1)), dma((2, 3, 2)), dma((2, 3, 2)),
        ],
        compiler_params=pltpu.CompilerParams(
            collective_id=0, has_side_effects=True, vmem_limit_bytes=VMEM_LIMIT
        ),
    )(*(pltpu.with_memory_space_constraint(a, pltpu.HBM) for a in (tokens, qkv_weight, tile_mask)))
    return out.reshape(clips, frames, rows, columns, width)


def solution(mesh):
    in_specs = (
        P("frame", None, "height", "width", None),
        P(None, ("frame", "height"), None),
        P("frame", None, None, None),
    )
    out_specs = P("frame", None, "height", "width", None)
    body = functools.partial(
        per_device, mesh.shape["frame"], mesh.shape["height"], mesh.shape["width"]
    )
    return jax.shard_map(body, mesh=mesh, in_specs=in_specs, out_specs=out_specs, check_vma=False)
```

```python
import functools
import math

import jax
import jax.numpy as jnp
from jax import lax
from jax.experimental import pallas as pl
from jax.experimental.pallas import tpu as pltpu
from jax.sharding import PartitionSpec as P

HEAD_DIM = 128
TILE = 4
VMEM_LIMIT = 54472 << 10
CUBE = TILE * TILE * TILE
MESH = pl.DeviceIdType.MESH

epsilon = 1e-06
QUERY, KEY, VALUE = 0, 1, 2


def kernel(
    n_h, n_w, x_ref, w_ref, tm_ref, o_ref,
    flags_ref, xs, xn, w_all, kbuf, vbuf, qbuf, mask,
    loc_sem, tok_s, tok_r, own_s, own_r, fwd_s, fwd_r, swap_s, swap_r, hgt_s, hgt_r, kvx_s, kvx_r,
):
    f, h, w = lax.axis_index("frame"), lax.axis_index("height"), lax.axis_index("width")
    f1 = f + 1 - 2 * (f % 2)
    f2 = f + 2 - 4 * ((f // 2) % 2)
    parity = f % 2
    side = w % 2
    rows = w_ref.shape[1]
    features = w_ref.shape[2]
    half = features // 2
    tokens = xn.shape[0] // 3
    span = 3 * CUBE
    slots = kbuf.shape[2] // span
    heads = kbuf.shape[0] // 2
    group_rows = heads * HEAD_DIM
    local = n_h * rows // HEAD_DIM
    tiles = tokens // CUBE
    halo = ((0, tiles - 1), (tiles - 1, 1))
    early_tokens = tokens + 2 * halo[0][1] * CUBE
    late_tokens = 2 * halo[1][1] * CUBE

    def halo_start(c, e):
        return (tokens, early_tokens)[c] + e * halo[c][1] * CUBE

    def place(owner_parity, group, row_parity, height):
        base = (owner_parity if group == 0 else 1 - owner_parity) * group_rows
        return pl.ds(pl.multiple_of(base + (row_parity * n_h + height) * rows, rows), rows)

    mine = place(parity, 0, parity, h)
    beside = place(parity, 0, 1 - parity, h)
    across = place(parity, 1, parity, h)
    corner = place(parity, 1, 1 - parity, h)

    def cols(s, p):
        at = p
        if s == QUERY:
            at = side if p == 0 else 1 - side
        return pl.ds(pl.multiple_of(at * half, half), half)

    def remote(src, dst, send, recv, target):
        return pltpu.make_async_remote_copy(
            src_ref=src, dst_ref=dst, send_sem=send, recv_sem=recv,
            device_id=target, device_id_type=MESH,
        )

    def to_frame(i):
        return ((f1, f2)[i], h, w)

    def own_copy(s, p, i):
        there = place(1 - parity, 0, parity, h) if i == 0 else across
        return remote(
            w_ref.at[s, :, cols(s, p)], w_all.at[s, there, cols(s, p)],
            own_s.at[s, p, i], own_r.at[s, p, i], to_frame(i),
        )

    def fwd_copy(s, i):
        if i == 1:
            src, there, at = beside, corner, cols(s, 0)
        else:
            src, there, at = across, place(1 - parity, 1, parity, h), cols(s, 1)
        return remote(w_all.at[s, src, at], w_all.at[s, there, at], fwd_s.at[s, i], fwd_r.at[s, i], to_frame(i))

    def swap_copy(i):
        part = w_all.at[QUERY, (beside, across)[i], cols(QUERY, i)]
        return remote(part, part, swap_s.at[i], swap_r.at[i], (f, h, w + 1 - 2 * side))

    def hgt_copy(s, piece, d):
        if piece == 0:
            src, dst = w_ref.at[s], w_all.at[s, mine]
        elif piece == 3:
            src = dst = w_all.at[s, corner]
        elif s != QUERY:
            src = dst = w_all.at[s, (beside, across)[piece - 1]]
        else:
            i = (piece - 1) % 3
            at = cols(s, i if piece < 3 else 1 - i)
            src = dst = w_all.at[s, (beside, across)[i], at]
        target = (f, lax.rem(h + d, n_h), w)
        return remote(src, dst, hgt_s.at[s, piece, d - 1], hgt_r.at[s, piece, d - 1], target)

    head_own = (parity * (2 * heads - local), local)
    head_beside = (local + parity * (heads - local), heads - local)
    head_other = ((1 - parity) * heads, heads)
    head_early = (parity * (heads - local), heads + local)
    head_late = ((1 - parity) * (heads + local), heads - local)

    kv_parts = ((head_early, *halo[0]), (head_early, *halo[1]), (head_late, 0, tiles))

    def kv_copy(which, part, up):
        buf = (kbuf, vbuf)[which]
        (first, count), start, length = kv_parts[part]
        slot = 1 if up or n_h == 2 else 2
        target = (f, h + 1 if up else h - 1, w)
        e = 0 if up else 1
        some = (pl.ds(first, count), pl.ds(start, length))
        src = buf.at[some + (pl.ds(0, span),)]
        dst = buf.at[some + (pl.ds(slot * span, span),)]
        return remote(src, dst, kvx_s.at[which, part, e], kvx_r.at[which, part, e], target)

    def tok_copy(e, c):
        target = (f, h, w + 1 if e == 0 else w - 1)
        at = pl.ds(halo[c][0] * TILE, halo[c][1] * TILE)
        return remote(x_ref.at[0, at], xs.at[1 + e, at], tok_s.at[e, c], tok_r.at[e, c], target)

    local_mask = pltpu.make_async_copy(tm_ref, flags_ref, loc_sem.at[4])
    local_x = pltpu.make_async_copy(x_ref.at[0], xs.at[0], loc_sem.at[0])
    local_w = [pltpu.make_async_copy(w_ref.at[s], w_all.at[s, mine], loc_sem.at[1 + s]) for s in range(3)]
    has_left, has_right = w > 0, w < n_w - 1
    has_below, has_above = h > 0, h < n_h - 1

    barrier = pltpu.get_barrier_semaphore()

    def greet(target):
        pl.semaphore_signal(barrier, inc=1, device_id=target, device_id_type=MESH)

    greet(to_frame(0))
    greet(to_frame(1))
    for d in range(1, n_h):
        greet((f, lax.rem(h + d, n_h), w))

    @pl.when(has_left)
    def _():
        greet((f, h, w - 1))

    @pl.when(has_right)
    def _():
        greet((f, h, w + 1))

    peers = n_h + 1 + has_left.astype(jnp.int32) + has_right.astype(jnp.int32)
    local_mask.start()
    local_x.start()
    for s in (KEY, VALUE, QUERY):
        local_w[s].start()
    pl.semaphore_wait(barrier, peers)

    def send_own(s):
        own_copy(s, 0, 0).start()
        own_copy(s, 1, 1).start()
        if s != QUERY:
            own_copy(s, 1, 0).start()
            own_copy(s, 0, 1).start()

    def wait_own(s):
        own_copy(s, 0, 0).wait_recv()
        own_copy(s, 1, 1).wait_recv()
        fwd_copy(s, 0).start()
        fwd_copy(s, 1).start()
        if s == QUERY:
            swap_copy(0).start()
            swap_copy(1).start()
        else:
            own_copy(s, 1, 0).wait_recv()
            own_copy(s, 0, 1).wait_recv()
        relay(s, 1, 2)

    def relay(s, *pieces):
        for piece in pieces:
            for d in range(1, n_h):
                hgt_copy(s, piece, d).start()

    def take_fwd(s):
        fwd_copy(s, 0).wait_recv()
        fwd_copy(s, 1).wait_recv()
        relay(s, 3)

    def take_swap(i):
        swap_copy(i).wait_recv()
        relay(QUERY, 4 + i)

    def wait_hgt(s, *pieces):
        for piece in pieces:
            for d in range(1, n_h):
                hgt_copy(s, piece, d).wait_recv()

    for s in (KEY, VALUE, QUERY):
        send_own(s)
    for c in range(2):
        @pl.when(has_right)
        def _():
            tok_copy(0, c).start()

        @pl.when(has_left)
        def _():
            tok_copy(1, c).start()

    for s in (KEY, VALUE, QUERY):
        relay(s, 0)

    local_mask.wait()
    total_h, total_w = tm_ref.shape[2], tm_ref.shape[3]
    shape = (tokens, slots * span)
    q_tile = lax.broadcasted_iota(jnp.int32, shape, 0) // CUBE
    block = lax.broadcasted_iota(jnp.int32, shape, 1) // CUBE
    for t in range(tiles):
        seen = jnp.zeros(shape, jnp.int32)
        for b in range(slots):
            if b == 0:
                row_h = h
            elif n_h == 2:
                row_h = 1 - h
            else:
                row_h = h - 1 if b == 1 else h + 1
            for c in range(3):
                col_w = w + (0, -1, 1)[c]
                inside = ((row_h >= 0) & (row_h < total_h) & (col_w >= 0) & (col_w < total_w)).astype(jnp.int32)
                at_h = jnp.minimum(jnp.maximum(row_h, 0), total_h - 1)
                at_w = jnp.minimum(jnp.maximum(col_w, 0), total_w - 1)
                flag = flags_ref[0, t, at_h, at_w] * inside
                seen = jnp.where(block == 3 * b + c, flag, seen)
        near = jnp.abs(q_tile - t) <= 1
        allowed = near & ((seen == 1) | ((block == 0) & (q_tile == t)))
        mask[:, t * slots * span : (t + 1) * slots * span] = jnp.where(
            allowed, jnp.float32(1.0), jnp.float32(0.0)
        ).astype(jnp.bfloat16)

    step = 64

    def normalise(c, frame, start, count):
        for t in range(count // step):
            each = step // (TILE * TILE)
            block = xs[c, frame + t * each : frame + (t + 1) * each].astype(jnp.float32).reshape(step, features)
            scale = lax.rsqrt(jnp.mean(block * block, -1, keepdims=True) + epsilon)
            xn[start + t * step : start + (t + 1) * step, :] = (block * scale).astype(jnp.bfloat16)

    def take_tokens(c):
        for e, here in ((0, has_left), (1, has_right)):
            start, chunk = halo_start(c, e), halo[c][1] * CUBE

            @pl.when(here)
            def _():
                tok_copy(e, c).wait_recv()
                normalise(1 + e, halo[c][0] * TILE, start, chunk)

            @pl.when(jnp.logical_not(here))
            def _():
                xn[start : start + chunk, :] = jnp.zeros((chunk, features), jnp.bfloat16)

    def head_norm(raw):
        return (raw * lax.rsqrt(jnp.mean(raw * raw, -1, keepdims=True) + epsilon)).astype(jnp.bfloat16)

    contract_last = (((1,), (1,)), ((), ()))

    blocks = [(t, 0, t * CUBE) for t in range(tiles)]
    for c in range(2):
        for e in range(2):
            blocks += [(halo[c][0] + t, 1 + e, halo_start(c, e) + t * CUBE) for t in range(halo[c][1])]

    def project(s, some, start, length):
        first, count = some
        place_rows = pl.ds(pl.multiple_of(first * HEAD_DIM, HEAD_DIM), count * HEAD_DIM)
        raw = lax.dot_general(
            xn[start : start + length, :], w_all[s, place_rows], contract_last, preferred_element_type=jnp.float32
        )
        for j in range(count):
            part = raw[:, j * HEAD_DIM : (j + 1) * HEAD_DIM]
            if s == QUERY:
                qbuf[first + j] = head_norm(part)
                continue
            buf = kbuf if s == KEY else vbuf
            part = head_norm(part) if s == KEY else part.astype(jnp.bfloat16)
            for t, c, at in blocks:
                if start <= at < start + length:
                    buf[first + j, t, c * CUBE : (c + 1) * CUBE, :] = part[at - start : at - start + CUBE]

    def send_kv(which, part):
        @pl.when(has_above)
        def _():
            kv_copy(which, part, True).start()

        @pl.when(has_below)
        def _():
            kv_copy(which, part, False).start()

    def wait_kv(*parts):
        for part in parts:
            for which in range(2):
                @pl.when(has_below)
                def _():
                    kv_copy(which, part, True).wait_recv()

                @pl.when(has_above)
                def _():
                    kv_copy(which, part, False).wait_recv()

    factor = HEAD_DIM ** (-0.5) * math.log2(math.e)
    pair = f // 2

    def attend(some):
        first, count = some

        for i in range(count):
            j = first + i
            keys = kbuf[j].reshape(tiles * slots * span, HEAD_DIM)
            values = vbuf[j].reshape(tiles * slots * span, HEAD_DIM)
            scores = lax.dot_general(qbuf[j], keys, contract_last, preferred_element_type=jnp.float32)
            upper = (j >= heads).astype(jnp.int32)
            group = lax.rem(pair + parity + upper, 2)
            at = (group * heads + j - upper * heads) * HEAD_DIM
            lanes = pl.ds(pl.multiple_of(at, HEAD_DIM), HEAD_DIM)
            for t in range(0, tiles, 2):
                queries = slice(t * CUBE, min(t + 2, tiles) * CUBE)
                near = slice(max(t - 1, 0) * slots * span, min(t + 3, tiles) * slots * span)
                weight = jnp.exp2(scores[queries, near] * factor).astype(jnp.bfloat16) * mask[queries, near]
                ones = jnp.ones((near.stop - near.start, HEAD_DIM), jnp.bfloat16)
                wide = jnp.concatenate([values[near], ones], 1)
                total = jnp.dot(weight, wide, preferred_element_type=jnp.float32)
                o_ref[queries, lanes] = (total[:, :HEAD_DIM] / total[:, HEAD_DIM:]).astype(o_ref.dtype)

    if n_h > 2:
        for edge, slot in ((h == 0, 1), (h == n_h - 1, 2)):
            @pl.when(edge)
            def _():
                at = slice(slot * span, (slot + 1) * span)
                blank = jnp.zeros((2 * heads, tiles, span, HEAD_DIM), jnp.bfloat16)
                kbuf[:, :, at] = blank
                vbuf[:, :, at] = blank

    local_x.wait()
    normalise(0, 0, 0, tokens)
    wait_own(KEY)
    local_w[KEY].wait()
    wait_hgt(KEY, 0, 1, 2)
    project(KEY, head_early, 0, tokens)
    wait_own(VALUE)
    take_tokens(0)
    project(KEY, head_early, tokens, early_tokens - tokens)
    send_kv(0, 0)
    local_w[VALUE].wait()
    wait_hgt(VALUE, 0, 1, 2)
    project(VALUE, head_early, 0, early_tokens)
    send_kv(1, 0)
    local_w[QUERY].wait()
    wait_hgt(QUERY, 0)
    project(QUERY, head_own, 0, tokens)
    wait_own(QUERY)
    take_tokens(1)
    project(KEY, head_early, early_tokens, late_tokens)
    send_kv(0, 1)
    project(VALUE, head_early, early_tokens, late_tokens)
    send_kv(1, 1)
    take_fwd(KEY)
    wait_kv(0, 1)
    attend(head_own)
    wait_hgt(KEY, 3)
    project(KEY, head_late, 0, 3 * tokens)
    take_swap(0)
    take_fwd(VALUE)
    send_kv(0, 2)
    wait_hgt(VALUE, 3)
    project(VALUE, head_late, 0, 3 * tokens)
    wait_hgt(QUERY, 1, 4)
    project(QUERY, head_beside, 0, tokens)
    take_swap(1)
    attend((head_beside[0], 1))
    take_fwd(QUERY)
    send_kv(1, 2)
    attend((head_beside[0] + 1, head_beside[1] - 1))
    wait_hgt(QUERY, 2, 5, 3)
    project(QUERY, head_other, 0, tokens)
    wait_kv(2)
    attend(head_other)

    for s in range(3):
        for i in range(2):
            own_copy(s, i, i).wait_send()
            fwd_copy(s, i).wait_send()
            if s != QUERY:
                own_copy(s, 1 - i, i).wait_send()
        for piece in range(6 if s == QUERY else 4):
            for d in range(1, n_h):
                hgt_copy(s, piece, d).wait_send()
    for i in range(2):
        swap_copy(i).wait_send()

    for c in range(2):
        @pl.when(has_right)
        def _():
            tok_copy(0, c).wait_send()

        @pl.when(has_left)
        def _():
            tok_copy(1, c).wait_send()

    for part in range(3):
        for which in range(2):
            @pl.when(has_above)
            def _():
                kv_copy(which, part, True).wait_send()

            @pl.when(has_below)
            def _():
                kv_copy(which, part, False).wait_send()


def per_device(n_f, n_h, n_w, tokens, qkv_weight, tile_mask):
    clips, frames, rows, columns, features = tokens.shape
    count = frames * rows * columns
    width = qkv_weight.shape[1] * n_f * n_h
    if n_f != 4 or n_h < 2 or n_w % 2 or clips != 1 or rows != TILE or columns != TILE:
        raise ValueError("unsupported placement")
    heads = width // HEAD_DIM
    slots = 2 if n_h == 2 else 3
    dma = pltpu.SemaphoreType.DMA
    out = pl.pallas_call(
        functools.partial(kernel, n_h, n_w),
        out_shape=jax.ShapeDtypeStruct((count, width), jnp.bfloat16),
        in_specs=[
            pl.BlockSpec(memory_space=pltpu.HBM),
            pl.BlockSpec(memory_space=pltpu.HBM),
            pl.BlockSpec(memory_space=pltpu.HBM),
        ],
        out_specs=pl.BlockSpec(memory_space=pltpu.VMEM),
        scratch_shapes=[
            pltpu.SMEM(tile_mask.shape, jnp.int32),
            pltpu.VMEM((3, frames, rows, columns, features), jnp.bfloat16),
            pltpu.VMEM((3 * count, features), jnp.bfloat16),
            pltpu.VMEM((3, width, features), jnp.bfloat16),
            pltpu.VMEM((heads, count // CUBE, slots * 3 * CUBE, HEAD_DIM), jnp.bfloat16),
            pltpu.VMEM((heads, count // CUBE, slots * 3 * CUBE, HEAD_DIM), jnp.bfloat16),
            pltpu.VMEM((heads, count, HEAD_DIM), jnp.bfloat16),
            pltpu.VMEM((count, slots * 3 * count), jnp.bfloat16),
            dma((5,)), dma((2, 2)), dma((2, 2)), dma((3, 2, 2)), dma((3, 2, 2)), dma((3, 2)), dma((3, 2)),
            dma((2,)), dma((2,)), dma((3, 6, n_h - 1)), dma((3, 6, n_h - 1)), dma((2, 3, 2)), dma((2, 3, 2)),
        ],
        compiler_params=pltpu.CompilerParams(
            collective_id=0, has_side_effects=True, vmem_limit_bytes=VMEM_LIMIT
        ),
    )(*(pltpu.with_memory_space_constraint(a, pltpu.HBM) for a in (tokens, qkv_weight, tile_mask)))
    return out.reshape(clips, frames, rows, columns, width)


def solution(mesh):
    in_specs = (
        P("frame", None, "height", "width", None),
        P(None, ("frame", "height"), None),
        P("frame", None, None, None),
    )
    out_specs = P("frame", None, "height", "width", None)
    body = functools.partial(
        per_device, mesh.shape["frame"], mesh.shape["height"], mesh.shape["width"]
    )
    return jax.shard_map(body, mesh=mesh, in_specs=in_specs, out_specs=out_specs, check_vma=False)
```

```python
import functools
import math

import jax
import jax.numpy as jnp
from jax import lax
from jax.experimental import pallas as pl
from jax.experimental.pallas import tpu as pltpu
from jax.sharding import PartitionSpec as P

HEAD_DIM = 128
TILE = 4
VMEM_LIMIT = 54472 << 10
CUBE = TILE * TILE * TILE
MESH = pl.DeviceIdType.MESH

epsilon = 1e-06
QUERY, KEY, VALUE = 0, 1, 2


def kernel(
    n_h, n_w, x_ref, w_ref, tm_ref, o_ref,
    flags_ref, xs, xn, w_all, kbuf, vbuf, qbuf, mask,
    loc_sem, tok_s, tok_r, own_s, own_r, fwd_s, fwd_r, swap_s, swap_r, hgt_s, hgt_r, kvx_s, kvx_r,
):
    f, h, w = lax.axis_index("frame"), lax.axis_index("height"), lax.axis_index("width")
    f1 = f + 1 - 2 * (f % 2)
    f2 = f + 2 - 4 * ((f // 2) % 2)
    parity = f % 2
    side = w % 2
    rows = w_ref.shape[1]
    features = w_ref.shape[2]
    half = features // 2
    tokens = xn.shape[0] // 3
    span = 3 * CUBE
    slots = kbuf.shape[2] // span
    heads = kbuf.shape[0] // 2
    group_rows = heads * HEAD_DIM
    local = n_h * rows // HEAD_DIM
    tiles = tokens // CUBE
    halo = ((0, tiles - 1), (tiles - 1, 1))
    early_tokens = tokens + 2 * halo[0][1] * CUBE
    late_tokens = 2 * halo[1][1] * CUBE

    def halo_start(c, e):
        return (tokens, early_tokens)[c] + e * halo[c][1] * CUBE

    def place(owner_parity, group, row_parity, height):
        base = (owner_parity if group == 0 else 1 - owner_parity) * group_rows
        return pl.ds(pl.multiple_of(base + (row_parity * n_h + height) * rows, rows), rows)

    mine = place(parity, 0, parity, h)
    beside = place(parity, 0, 1 - parity, h)
    across = place(parity, 1, parity, h)
    corner = place(parity, 1, 1 - parity, h)

    def cols(s, p):
        at = p
        if s == QUERY:
            at = side if p == 0 else 1 - side
        return pl.ds(pl.multiple_of(at * half, half), half)

    def remote(src, dst, send, recv, target):
        return pltpu.make_async_remote_copy(
            src_ref=src, dst_ref=dst, send_sem=send, recv_sem=recv,
            device_id=target, device_id_type=MESH,
        )

    def to_frame(i):
        return ((f1, f2)[i], h, w)

    def own_copy(s, p, i):
        there = place(1 - parity, 0, parity, h) if i == 0 else across
        return remote(
            w_ref.at[s, :, cols(s, p)], w_all.at[s, there, cols(s, p)],
            own_s.at[s, p, i], own_r.at[s, p, i], to_frame(i),
        )

    def fwd_copy(s, i):
        if i == 1:
            src, there, at = beside, corner, cols(s, 0)
        else:
            src, there, at = across, place(1 - parity, 1, parity, h), cols(s, 1)
        return remote(w_all.at[s, src, at], w_all.at[s, there, at], fwd_s.at[s, i], fwd_r.at[s, i], to_frame(i))

    def swap_copy(i):
        part = w_all.at[QUERY, (beside, across)[i], cols(QUERY, i)]
        return remote(part, part, swap_s.at[i], swap_r.at[i], (f, h, w + 1 - 2 * side))

    def hgt_copy(s, piece, d):
        if piece == 0:
            src, dst = w_ref.at[s], w_all.at[s, mine]
        elif piece == 3:
            src = dst = w_all.at[s, corner]
        elif s != QUERY:
            src = dst = w_all.at[s, (beside, across)[piece - 1]]
        else:
            i = (piece - 1) % 3
            at = cols(s, i if piece < 3 else 1 - i)
            src = dst = w_all.at[s, (beside, across)[i], at]
        target = (f, lax.rem(h + d, n_h), w)
        return remote(src, dst, hgt_s.at[s, piece, d - 1], hgt_r.at[s, piece, d - 1], target)

    head_own = (parity * (2 * heads - local), local)
    head_beside = (local + parity * (heads - local), heads - local)
    head_other = ((1 - parity) * heads, heads)
    head_early = (parity * (heads - local), heads + local)
    head_late = ((1 - parity) * (heads + local), heads - local)

    kv_parts = ((head_early, *halo[0]), (head_early, *halo[1]), (head_late, 0, tiles))

    def kv_copy(which, part, up):
        buf = (kbuf, vbuf)[which]
        (first, count), start, length = kv_parts[part]
        slot = 1 if up or n_h == 2 else 2
        target = (f, h + 1 if up else h - 1, w)
        e = 0 if up else 1
        some = (pl.ds(first, count), pl.ds(start, length))
        src = buf.at[some + (pl.ds(0, span),)]
        dst = buf.at[some + (pl.ds(slot * span, span),)]
        return remote(src, dst, kvx_s.at[which, part, e], kvx_r.at[which, part, e], target)

    def tok_copy(e, c):
        target = (f, h, w + 1 if e == 0 else w - 1)
        at = pl.ds(halo[c][0] * TILE, halo[c][1] * TILE)
        return remote(x_ref.at[0, at], xs.at[1 + e, at], tok_s.at[e, c], tok_r.at[e, c], target)

    local_mask = pltpu.make_async_copy(tm_ref, flags_ref, loc_sem.at[4])
    local_x = pltpu.make_async_copy(x_ref.at[0], xs.at[0], loc_sem.at[0])
    local_w = [pltpu.make_async_copy(w_ref.at[s], w_all.at[s, mine], loc_sem.at[1 + s]) for s in range(3)]
    has_left, has_right = w > 0, w < n_w - 1
    has_below, has_above = h > 0, h < n_h - 1

    barrier = pltpu.get_barrier_semaphore()

    def greet(target):
        pl.semaphore_signal(barrier, inc=1, device_id=target, device_id_type=MESH)

    greet(to_frame(0))
    greet(to_frame(1))
    for d in range(1, n_h):
        greet((f, lax.rem(h + d, n_h), w))

    @pl.when(has_left)
    def _():
        greet((f, h, w - 1))

    @pl.when(has_right)
    def _():
        greet((f, h, w + 1))

    peers = n_h + 1 + has_left.astype(jnp.int32) + has_right.astype(jnp.int32)
    local_mask.start()
    local_x.start()
    for s in (KEY, VALUE, QUERY):
        local_w[s].start()
    pl.semaphore_wait(barrier, peers)

    def send_own(s):
        own_copy(s, 0, 0).start()
        own_copy(s, 1, 1).start()
        if s != QUERY:
            own_copy(s, 1, 0).start()
            own_copy(s, 0, 1).start()

    def wait_own(s):
        own_copy(s, 0, 0).wait_recv()
        own_copy(s, 1, 1).wait_recv()
        fwd_copy(s, 0).start()
        fwd_copy(s, 1).start()
        if s == QUERY:
            swap_copy(0).start()
            swap_copy(1).start()
        else:
            own_copy(s, 1, 0).wait_recv()
            own_copy(s, 0, 1).wait_recv()
        relay(s, 1, 2)

    def relay(s, *pieces):
        for piece in pieces:
            for d in range(1, n_h):
                hgt_copy(s, piece, d).start()

    def take_fwd(s):
        fwd_copy(s, 0).wait_recv()
        fwd_copy(s, 1).wait_recv()
        relay(s, 3)

    def take_swap(i):
        swap_copy(i).wait_recv()
        relay(QUERY, 4 + i)

    def wait_hgt(s, *pieces):
        for piece in pieces:
            for d in range(1, n_h):
                hgt_copy(s, piece, d).wait_recv()

    for s in (KEY, VALUE, QUERY):
        send_own(s)
    for c in range(2):
        @pl.when(has_right)
        def _():
            tok_copy(0, c).start()

        @pl.when(has_left)
        def _():
            tok_copy(1, c).start()

    for s in (KEY, VALUE, QUERY):
        relay(s, 0)

    local_mask.wait()
    total_h, total_w = tm_ref.shape[2], tm_ref.shape[3]
    shape = (tokens, slots * span)
    q_tile = lax.broadcasted_iota(jnp.int32, shape, 0) // CUBE
    block = lax.broadcasted_iota(jnp.int32, shape, 1) // CUBE
    for t in range(tiles):
        seen = jnp.zeros(shape, jnp.int32)
        for b in range(slots):
            if b == 0:
                row_h = h
            elif n_h == 2:
                row_h = 1 - h
            else:
                row_h = h - 1 if b == 1 else h + 1
            for c in range(3):
                col_w = w + (0, -1, 1)[c]
                inside = ((row_h >= 0) & (row_h < total_h) & (col_w >= 0) & (col_w < total_w)).astype(jnp.int32)
                at_h = jnp.minimum(jnp.maximum(row_h, 0), total_h - 1)
                at_w = jnp.minimum(jnp.maximum(col_w, 0), total_w - 1)
                flag = flags_ref[0, t, at_h, at_w] * inside
                seen = jnp.where(block == 3 * b + c, flag, seen)
        near = jnp.abs(q_tile - t) <= 1
        allowed = near & ((seen == 1) | ((block == 0) & (q_tile == t)))
        mask[:, t * slots * span : (t + 1) * slots * span] = jnp.where(
            allowed, jnp.float32(1.0), jnp.float32(0.0)
        ).astype(jnp.bfloat16)

    step = 64

    def normalise(c, frame, start, count):
        for t in range(count // step):
            each = step // (TILE * TILE)
            block = xs[c, frame + t * each : frame + (t + 1) * each].astype(jnp.float32).reshape(step, features)
            scale = lax.rsqrt(jnp.mean(block * block, -1, keepdims=True) + epsilon)
            xn[start + t * step : start + (t + 1) * step, :] = (block * scale).astype(jnp.bfloat16)

    def take_tokens(c):
        for e, here in ((0, has_left), (1, has_right)):
            start, chunk = halo_start(c, e), halo[c][1] * CUBE

            @pl.when(here)
            def _():
                tok_copy(e, c).wait_recv()
                normalise(1 + e, halo[c][0] * TILE, start, chunk)

            @pl.when(jnp.logical_not(here))
            def _():
                xn[start : start + chunk, :] = jnp.zeros((chunk, features), jnp.bfloat16)

    def head_norm(raw):
        return (raw * lax.rsqrt(jnp.mean(raw * raw, -1, keepdims=True) + epsilon)).astype(jnp.bfloat16)

    contract_last = (((1,), (1,)), ((), ()))

    blocks = [(t, 0, t * CUBE) for t in range(tiles)]
    for c in range(2):
        for e in range(2):
            blocks += [(halo[c][0] + t, 1 + e, halo_start(c, e) + t * CUBE) for t in range(halo[c][1])]

    def project(s, some, start, length):
        first, count = some
        wide = 2 if count % 2 == 0 else 1 if s != QUERY else count

        def body(i, carry):
            head = first + i * wide
            place_rows = pl.ds(pl.multiple_of(head * HEAD_DIM, HEAD_DIM), wide * HEAD_DIM)
            raw = lax.dot_general(
                xn[start : start + length, :], w_all[s, place_rows], contract_last, preferred_element_type=jnp.float32
            )
            for j in range(wide):
                part = raw[:, j * HEAD_DIM : (j + 1) * HEAD_DIM]
                if s == QUERY:
                    qbuf[head + j] = head_norm(part)
                    continue
                buf = kbuf if s == KEY else vbuf
                part = head_norm(part) if s == KEY else part.astype(jnp.bfloat16)
                for t, c, at in blocks:
                    if start <= at < start + length:
                        buf[head + j, t, c * CUBE : (c + 1) * CUBE, :] = part[at - start : at - start + CUBE]
            return carry

        if count == wide:
            body(0, 0)
        else:
            lax.fori_loop(0, count // wide, body, 0)

    def send_kv(which, part):
        @pl.when(has_above)
        def _():
            kv_copy(which, part, True).start()

        @pl.when(has_below)
        def _():
            kv_copy(which, part, False).start()

    def wait_kv(*parts):
        for part in parts:
            for which in range(2):
                @pl.when(has_below)
                def _():
                    kv_copy(which, part, True).wait_recv()

                @pl.when(has_above)
                def _():
                    kv_copy(which, part, False).wait_recv()

    factor = HEAD_DIM ** (-0.5) * math.log2(math.e)
    pair = f // 2

    def attend(some):
        first, count = some

        for i in range(count):
            j = first + i
            keys = kbuf[j].reshape(tiles * slots * span, HEAD_DIM)
            values = vbuf[j].reshape(tiles * slots * span, HEAD_DIM)
            scores = lax.dot_general(qbuf[j], keys, contract_last, preferred_element_type=jnp.float32)
            upper = (j >= heads).astype(jnp.int32)
            group = lax.rem(pair + parity + upper, 2)
            at = (group * heads + j - upper * heads) * HEAD_DIM
            lanes = pl.ds(pl.multiple_of(at, HEAD_DIM), HEAD_DIM)
            for t in range(0, tiles, 2):
                queries = slice(t * CUBE, min(t + 2, tiles) * CUBE)
                near = slice(max(t - 1, 0) * slots * span, min(t + 3, tiles) * slots * span)
                weight = jnp.exp2(scores[queries, near] * factor).astype(jnp.bfloat16) * mask[queries, near]
                ones = jnp.ones((near.stop - near.start, HEAD_DIM), jnp.bfloat16)
                wide = jnp.concatenate([values[near], ones], 1)
                total = jnp.dot(weight, wide, preferred_element_type=jnp.float32)
                o_ref[queries, lanes] = (total[:, :HEAD_DIM] / total[:, HEAD_DIM:]).astype(o_ref.dtype)

    if n_h > 2:
        for edge, slot in ((h == 0, 1), (h == n_h - 1, 2)):
            @pl.when(edge)
            def _():
                at = slice(slot * span, (slot + 1) * span)
                blank = jnp.zeros((2 * heads, tiles, span, HEAD_DIM), jnp.bfloat16)
                kbuf[:, :, at] = blank
                vbuf[:, :, at] = blank

    local_x.wait()
    normalise(0, 0, 0, tokens)
    wait_own(KEY)
    local_w[KEY].wait()
    wait_hgt(KEY, 0, 1, 2)
    project(KEY, head_early, 0, tokens)
    wait_own(VALUE)
    take_tokens(0)
    project(KEY, head_early, tokens, early_tokens - tokens)
    send_kv(0, 0)
    local_w[VALUE].wait()
    wait_hgt(VALUE, 0, 1, 2)
    project(VALUE, head_early, 0, early_tokens)
    send_kv(1, 0)
    local_w[QUERY].wait()
    wait_hgt(QUERY, 0)
    project(QUERY, head_own, 0, tokens)
    wait_own(QUERY)
    take_tokens(1)
    project(KEY, head_early, early_tokens, late_tokens)
    send_kv(0, 1)
    project(VALUE, head_early, early_tokens, late_tokens)
    send_kv(1, 1)
    take_fwd(KEY)
    wait_kv(0, 1)
    attend(head_own)
    wait_hgt(KEY, 3)
    project(KEY, head_late, 0, 3 * tokens)
    take_swap(0)
    take_fwd(VALUE)
    send_kv(0, 2)
    wait_hgt(VALUE, 3)
    project(VALUE, head_late, 0, 3 * tokens)
    take_swap(1)
    take_fwd(QUERY)
    wait_hgt(QUERY, 1, 4)
    project(QUERY, head_beside, 0, tokens)
    send_kv(1, 2)
    attend(head_beside)
    wait_hgt(QUERY, 2, 5, 3)
    project(QUERY, head_other, 0, tokens)
    wait_kv(2)
    attend(head_other)

    for s in range(3):
        for i in range(2):
            own_copy(s, i, i).wait_send()
            fwd_copy(s, i).wait_send()
            if s != QUERY:
                own_copy(s, 1 - i, i).wait_send()
        for piece in range(6 if s == QUERY else 4):
            for d in range(1, n_h):
                hgt_copy(s, piece, d).wait_send()
    for i in range(2):
        swap_copy(i).wait_send()

    for c in range(2):
        @pl.when(has_right)
        def _():
            tok_copy(0, c).wait_send()

        @pl.when(has_left)
        def _():
            tok_copy(1, c).wait_send()

    for part in range(3):
        for which in range(2):
            @pl.when(has_above)
            def _():
                kv_copy(which, part, True).wait_send()

            @pl.when(has_below)
            def _():
                kv_copy(which, part, False).wait_send()


def per_device(n_f, n_h, n_w, tokens, qkv_weight, tile_mask):
    clips, frames, rows, columns, features = tokens.shape
    count = frames * rows * columns
    width = qkv_weight.shape[1] * n_f * n_h
    if n_f != 4 or n_h < 2 or n_w % 2 or clips != 1 or rows != TILE or columns != TILE:
        raise ValueError("unsupported placement")
    heads = width // HEAD_DIM
    slots = 2 if n_h == 2 else 3
    dma = pltpu.SemaphoreType.DMA
    out = pl.pallas_call(
        functools.partial(kernel, n_h, n_w),
        out_shape=jax.ShapeDtypeStruct((count, width), jnp.bfloat16),
        in_specs=[
            pl.BlockSpec(memory_space=pltpu.HBM),
            pl.BlockSpec(memory_space=pltpu.HBM),
            pl.BlockSpec(memory_space=pltpu.HBM),
        ],
        out_specs=pl.BlockSpec(memory_space=pltpu.VMEM),
        scratch_shapes=[
            pltpu.SMEM(tile_mask.shape, jnp.int32),
            pltpu.VMEM((3, frames, rows, columns, features), jnp.bfloat16),
            pltpu.VMEM((3 * count, features), jnp.bfloat16),
            pltpu.VMEM((3, width, features), jnp.bfloat16),
            pltpu.VMEM((heads, count // CUBE, slots * 3 * CUBE, HEAD_DIM), jnp.bfloat16),
            pltpu.VMEM((heads, count // CUBE, slots * 3 * CUBE, HEAD_DIM), jnp.bfloat16),
            pltpu.VMEM((heads, count, HEAD_DIM), jnp.bfloat16),
            pltpu.VMEM((count, slots * 3 * count), jnp.bfloat16),
            dma((5,)), dma((2, 2)), dma((2, 2)), dma((3, 2, 2)), dma((3, 2, 2)), dma((3, 2)), dma((3, 2)),
            dma((2,)), dma((2,)), dma((3, 6, n_h - 1)), dma((3, 6, n_h - 1)), dma((2, 3, 2)), dma((2, 3, 2)),
        ],
        compiler_params=pltpu.CompilerParams(
            collective_id=0, has_side_effects=True, vmem_limit_bytes=VMEM_LIMIT
        ),
    )(*(pltpu.with_memory_space_constraint(a, pltpu.HBM) for a in (tokens, qkv_weight, tile_mask)))
    return out.reshape(clips, frames, rows, columns, width)


def solution(mesh):
    in_specs = (
        P("frame", None, "height", "width", None),
        P(None, ("frame", "height"), None),
        P("frame", None, None, None),
    )
    out_specs = P("frame", None, "height", "width", None)
    body = functools.partial(
        per_device, mesh.shape["frame"], mesh.shape["height"], mesh.shape["width"]
    )
    return jax.shard_map(body, mesh=mesh, in_specs=in_specs, out_specs=out_specs, check_vma=False)
```

```python
import functools
import math

import jax
import jax.numpy as jnp
from jax import lax
from jax.experimental import pallas as pl
from jax.experimental.pallas import tpu as pltpu
from jax.sharding import PartitionSpec as P

HEAD_DIM = 128
TILE = 4
VMEM_LIMIT = 54472 << 10
CUBE = TILE * TILE * TILE
MESH = pl.DeviceIdType.MESH

epsilon = 1e-06
QUERY, KEY, VALUE = 0, 1, 2


def kernel(
    n_h, n_w, x_ref, w_ref, tm_ref, o_ref,
    flags_ref, xs, xn, w_all, kbuf, vbuf, qbuf, mask,
    loc_sem, tok_s, tok_r, own_s, own_r, fwd_s, fwd_r, swap_s, swap_r, hgt_s, hgt_r, kvx_s, kvx_r,
):
    f, h, w = lax.axis_index("frame"), lax.axis_index("height"), lax.axis_index("width")
    f1 = f + 1 - 2 * (f % 2)
    f2 = f + 2 - 4 * ((f // 2) % 2)
    parity = f % 2
    side = w % 2
    rows = w_ref.shape[1]
    features = w_ref.shape[2]
    half = features // 2
    tokens = xn.shape[0] // 3
    span = 3 * CUBE
    slots = kbuf.shape[2] // span
    heads = kbuf.shape[0] // 2
    group_rows = heads * HEAD_DIM
    local = n_h * rows // HEAD_DIM
    tiles = tokens // CUBE
    halo = ((0, tiles - 1), (tiles - 1, 1))
    early_tokens = tokens + 2 * halo[0][1] * CUBE
    late_tokens = 2 * halo[1][1] * CUBE

    def halo_start(c, e):
        return (tokens, early_tokens)[c] + e * halo[c][1] * CUBE

    def place(owner_parity, group, row_parity, height):
        base = (owner_parity if group == 0 else 1 - owner_parity) * group_rows
        return pl.ds(pl.multiple_of(base + (row_parity * n_h + height) * rows, rows), rows)

    mine = place(parity, 0, parity, h)
    beside = place(parity, 0, 1 - parity, h)
    across = place(parity, 1, parity, h)
    corner = place(parity, 1, 1 - parity, h)

    def cols(s, p):
        at = p
        if s == QUERY:
            at = side if p == 0 else 1 - side
        return pl.ds(pl.multiple_of(at * half, half), half)

    def remote(src, dst, send, recv, target):
        return pltpu.make_async_remote_copy(
            src_ref=src, dst_ref=dst, send_sem=send, recv_sem=recv,
            device_id=target, device_id_type=MESH,
        )

    def to_frame(i):
        return ((f1, f2)[i], h, w)

    def own_copy(s, p, i):
        there = place(1 - parity, 0, parity, h) if i == 0 else across
        return remote(
            w_ref.at[s, :, cols(s, p)], w_all.at[s, there, cols(s, p)],
            own_s.at[s, p, i], own_r.at[s, p, i], to_frame(i),
        )

    def fwd_copy(s, i):
        if i == 1:
            src, there, at = beside, corner, cols(s, 0)
        else:
            src, there, at = across, place(1 - parity, 1, parity, h), cols(s, 1)
        return remote(w_all.at[s, src, at], w_all.at[s, there, at], fwd_s.at[s, i], fwd_r.at[s, i], to_frame(i))

    def swap_copy(i):
        part = w_all.at[QUERY, (beside, across)[i], cols(QUERY, i)]
        return remote(part, part, swap_s.at[i], swap_r.at[i], (f, h, w + 1 - 2 * side))

    def hgt_copy(s, piece, d):
        if piece == 0:
            src, dst = w_ref.at[s], w_all.at[s, mine]
        elif piece == 3:
            src = dst = w_all.at[s, corner]
        elif s != QUERY:
            src = dst = w_all.at[s, (beside, across)[piece - 1]]
        else:
            i = (piece - 1) % 3
            at = cols(s, i if piece < 3 else 1 - i)
            src = dst = w_all.at[s, (beside, across)[i], at]
        target = (f, lax.rem(h + d, n_h), w)
        return remote(src, dst, hgt_s.at[s, piece, d - 1], hgt_r.at[s, piece, d - 1], target)

    head_own = (parity * (2 * heads - local), local)
    head_beside = (local + parity * (heads - local), heads - local)
    head_other = ((1 - parity) * heads, heads)
    head_early = (parity * (heads - local), heads + local)
    head_late = ((1 - parity) * (heads + local), heads - local)

    kv_parts = ((head_early, *halo[0]), (head_early, *halo[1]), (head_late, 0, tiles))

    def kv_copy(which, part, up):
        buf = (kbuf, vbuf)[which]
        (first, count), start, length = kv_parts[part]
        slot = 1 if up or n_h == 2 else 2
        target = (f, h + 1 if up else h - 1, w)
        e = 0 if up else 1
        some = (pl.ds(first, count), pl.ds(start, length))
        src = buf.at[some + (pl.ds(0, span),)]
        dst = buf.at[some + (pl.ds(slot * span, span),)]
        return remote(src, dst, kvx_s.at[which, part, e], kvx_r.at[which, part, e], target)

    def tok_copy(e, c):
        target = (f, h, w + 1 if e == 0 else w - 1)
        at = pl.ds(halo[c][0] * TILE, halo[c][1] * TILE)
        return remote(x_ref.at[0, at], xs.at[1 + e, at], tok_s.at[e, c], tok_r.at[e, c], target)

    local_mask = pltpu.make_async_copy(tm_ref, flags_ref, loc_sem.at[4])
    local_x = pltpu.make_async_copy(x_ref.at[0], xs.at[0], loc_sem.at[0])
    local_w = [pltpu.make_async_copy(w_ref.at[s], w_all.at[s, mine], loc_sem.at[1 + s]) for s in range(3)]
    has_left, has_right = w > 0, w < n_w - 1
    has_below, has_above = h > 0, h < n_h - 1

    barrier = pltpu.get_barrier_semaphore()

    def greet(target):
        pl.semaphore_signal(barrier, inc=1, device_id=target, device_id_type=MESH)

    greet(to_frame(0))
    greet(to_frame(1))
    for d in range(1, n_h):
        greet((f, lax.rem(h + d, n_h), w))

    @pl.when(has_left)
    def _():
        greet((f, h, w - 1))

    @pl.when(has_right)
    def _():
        greet((f, h, w + 1))

    peers = n_h + 1 + has_left.astype(jnp.int32) + has_right.astype(jnp.int32)
    local_mask.start()
    local_x.start()
    for s in (KEY, VALUE, QUERY):
        local_w[s].start()
    pl.semaphore_wait(barrier, peers)

    def send_own(s):
        own_copy(s, 0, 0).start()
        own_copy(s, 1, 1).start()
        if s != QUERY:
            own_copy(s, 1, 0).start()
            own_copy(s, 0, 1).start()

    def wait_own(s):
        own_copy(s, 0, 0).wait_recv()
        own_copy(s, 1, 1).wait_recv()
        fwd_copy(s, 0).start()
        fwd_copy(s, 1).start()
        if s == QUERY:
            swap_copy(0).start()
            swap_copy(1).start()
        else:
            own_copy(s, 1, 0).wait_recv()
            own_copy(s, 0, 1).wait_recv()
        relay(s, 1, 2)

    def relay(s, *pieces):
        for piece in pieces:
            for d in range(1, n_h):
                hgt_copy(s, piece, d).start()

    def take_fwd(s):
        fwd_copy(s, 0).wait_recv()
        fwd_copy(s, 1).wait_recv()
        relay(s, 3)

    def take_swap(i):
        swap_copy(i).wait_recv()
        relay(QUERY, 4 + i)

    def wait_hgt(s, *pieces):
        for piece in pieces:
            for d in range(1, n_h):
                hgt_copy(s, piece, d).wait_recv()

    for s in (KEY, VALUE, QUERY):
        send_own(s)
    for c in range(2):
        @pl.when(has_right)
        def _():
            tok_copy(0, c).start()

        @pl.when(has_left)
        def _():
            tok_copy(1, c).start()

    for s in (KEY, VALUE, QUERY):
        relay(s, 0)

    local_mask.wait()
    total_h, total_w = tm_ref.shape[2], tm_ref.shape[3]
    shape = (tokens, slots * span)
    q_tile = lax.broadcasted_iota(jnp.int32, shape, 0) // CUBE
    block = lax.broadcasted_iota(jnp.int32, shape, 1) // CUBE
    for t in range(tiles):
        seen = jnp.zeros(shape, jnp.int32)
        for b in range(slots):
            if b == 0:
                row_h = h
            elif n_h == 2:
                row_h = 1 - h
            else:
                row_h = h - 1 if b == 1 else h + 1
            for c in range(3):
                col_w = w + (0, -1, 1)[c]
                inside = ((row_h >= 0) & (row_h < total_h) & (col_w >= 0) & (col_w < total_w)).astype(jnp.int32)
                at_h = jnp.minimum(jnp.maximum(row_h, 0), total_h - 1)
                at_w = jnp.minimum(jnp.maximum(col_w, 0), total_w - 1)
                flag = flags_ref[0, t, at_h, at_w] * inside
                seen = jnp.where(block == 3 * b + c, flag, seen)
        near = jnp.abs(q_tile - t) <= 1
        allowed = near & ((seen == 1) | ((block == 0) & (q_tile == t)))
        mask[:, t * slots * span : (t + 1) * slots * span] = jnp.where(
            allowed, jnp.float32(1.0), jnp.float32(0.0)
        ).astype(jnp.bfloat16)

    step = 64

    def normalise(c, frame, start, count):
        for t in range(count // step):
            each = step // (TILE * TILE)
            block = xs[c, frame + t * each : frame + (t + 1) * each].astype(jnp.float32).reshape(step, features)
            scale = lax.rsqrt(jnp.mean(block * block, -1, keepdims=True) + epsilon)
            xn[start + t * step : start + (t + 1) * step, :] = (block * scale).astype(jnp.bfloat16)

    def take_tokens(c):
        for e, here in ((0, has_left), (1, has_right)):
            start, chunk = halo_start(c, e), halo[c][1] * CUBE

            @pl.when(here)
            def _():
                tok_copy(e, c).wait_recv()
                normalise(1 + e, halo[c][0] * TILE, start, chunk)

            @pl.when(jnp.logical_not(here))
            def _():
                xn[start : start + chunk, :] = jnp.zeros((chunk, features), jnp.bfloat16)

    def head_norm(raw):
        return (raw * lax.rsqrt(jnp.mean(raw * raw, -1, keepdims=True) + epsilon)).astype(jnp.bfloat16)

    contract_last = (((1,), (1,)), ((), ()))

    blocks = [(t, 0, t * CUBE) for t in range(tiles)]
    for c in range(2):
        for e in range(2):
            blocks += [(halo[c][0] + t, 1 + e, halo_start(c, e) + t * CUBE) for t in range(halo[c][1])]

    def project(s, some, start, length):
        first, count = some
        wide = 2 if count % 2 == 0 else 1 if s != QUERY else count

        def body(i, carry):
            head = first + i * wide
            place_rows = pl.ds(pl.multiple_of(head * HEAD_DIM, HEAD_DIM), wide * HEAD_DIM)
            raw = lax.dot_general(
                xn[start : start + length, :], w_all[s, place_rows], contract_last, preferred_element_type=jnp.float32
            )
            for j in range(wide):
                part = raw[:, j * HEAD_DIM : (j + 1) * HEAD_DIM]
                if s == QUERY:
                    qbuf[head + j] = head_norm(part)
                    continue
                buf = kbuf if s == KEY else vbuf
                part = head_norm(part) if s == KEY else part.astype(jnp.bfloat16)
                for t, c, at in blocks:
                    if start <= at < start + length:
                        buf[head + j, t, c * CUBE : (c + 1) * CUBE, :] = part[at - start : at - start + CUBE]
            return carry

        if count == wide:
            body(0, 0)
        else:
            lax.fori_loop(0, count // wide, body, 0)

    def send_kv(which, part):
        @pl.when(has_above)
        def _():
            kv_copy(which, part, True).start()

        @pl.when(has_below)
        def _():
            kv_copy(which, part, False).start()

    def wait_kv(*parts):
        for part in parts:
            for which in range(2):
                @pl.when(has_below)
                def _():
                    kv_copy(which, part, True).wait_recv()

                @pl.when(has_above)
                def _():
                    kv_copy(which, part, False).wait_recv()

    factor = HEAD_DIM ** (-0.5) * math.log2(math.e)
    pair = f // 2

    def attend(some):
        first, count = some

        for i in range(count):
            j = first + i
            keys = kbuf[j].reshape(tiles * slots * span, HEAD_DIM)
            values = vbuf[j].reshape(tiles * slots * span, HEAD_DIM)
            scores = lax.dot_general(qbuf[j], keys, contract_last, preferred_element_type=jnp.float32)
            upper = (j >= heads).astype(jnp.int32)
            group = lax.rem(pair + parity + upper, 2)
            at = (group * heads + j - upper * heads) * HEAD_DIM
            lanes = pl.ds(pl.multiple_of(at, HEAD_DIM), HEAD_DIM)
            for t in range(0, tiles, 2):
                queries = slice(t * CUBE, min(t + 2, tiles) * CUBE)
                near = slice(max(t - 1, 0) * slots * span, min(t + 3, tiles) * slots * span)
                weight = jnp.exp2(scores[queries, near] * factor).astype(jnp.bfloat16) * mask[queries, near]
                ones = jnp.ones((near.stop - near.start, HEAD_DIM), jnp.bfloat16)
                wide = jnp.concatenate([values[near], ones], 1)
                total = jnp.dot(weight, wide, preferred_element_type=jnp.float32)
                o_ref[queries, lanes] = (total[:, :HEAD_DIM] / total[:, HEAD_DIM:]).astype(o_ref.dtype)

    if n_h > 2:
        for edge, slot in ((h == 0, 1), (h == n_h - 1, 2)):
            @pl.when(edge)
            def _():
                at = slice(slot * span, (slot + 1) * span)
                blank = jnp.zeros((2 * heads, tiles, span, HEAD_DIM), jnp.bfloat16)
                kbuf[:, :, at] = blank
                vbuf[:, :, at] = blank

    local_x.wait()
    normalise(0, 0, 0, tokens)
    wait_own(KEY)
    local_w[KEY].wait()
    wait_hgt(KEY, 0, 1, 2)
    project(KEY, head_early, 0, tokens)
    wait_own(VALUE)
    take_tokens(0)
    project(KEY, head_early, tokens, early_tokens - tokens)
    send_kv(0, 0)
    local_w[VALUE].wait()
    wait_hgt(VALUE, 0, 1, 2)
    project(VALUE, head_early, 0, early_tokens)
    send_kv(1, 0)
    local_w[QUERY].wait()
    wait_hgt(QUERY, 0)
    project(QUERY, head_own, 0, tokens)
    wait_own(QUERY)
    take_tokens(1)
    project(KEY, head_early, early_tokens, late_tokens)
    send_kv(0, 1)
    project(VALUE, head_early, early_tokens, late_tokens)
    send_kv(1, 1)
    take_fwd(KEY)
    wait_hgt(KEY, 3)
    project(KEY, head_late, 0, 3 * tokens)
    take_fwd(VALUE)
    take_swap(0)
    wait_kv(0, 1)
    attend(head_own)
    send_kv(0, 2)
    wait_hgt(VALUE, 3)
    project(VALUE, head_late, 0, 3 * tokens)
    take_swap(1)
    take_fwd(QUERY)
    wait_hgt(QUERY, 1, 4)
    project(QUERY, head_beside, 0, tokens)
    send_kv(1, 2)
    attend(head_beside)
    wait_hgt(QUERY, 2, 5, 3)
    project(QUERY, head_other, 0, tokens)
    wait_kv(2)
    attend(head_other)

    for s in range(3):
        for i in range(2):
            own_copy(s, i, i).wait_send()
            fwd_copy(s, i).wait_send()
            if s != QUERY:
                own_copy(s, 1 - i, i).wait_send()
        for piece in range(6 if s == QUERY else 4):
            for d in range(1, n_h):
                hgt_copy(s, piece, d).wait_send()
    for i in range(2):
        swap_copy(i).wait_send()

    for c in range(2):
        @pl.when(has_right)
        def _():
            tok_copy(0, c).wait_send()

        @pl.when(has_left)
        def _():
            tok_copy(1, c).wait_send()

    for part in range(3):
        for which in range(2):
            @pl.when(has_above)
            def _():
                kv_copy(which, part, True).wait_send()

            @pl.when(has_below)
            def _():
                kv_copy(which, part, False).wait_send()


def per_device(n_f, n_h, n_w, tokens, qkv_weight, tile_mask):
    clips, frames, rows, columns, features = tokens.shape
    count = frames * rows * columns
    width = qkv_weight.shape[1] * n_f * n_h
    if n_f != 4 or n_h < 2 or n_w % 2 or clips != 1 or rows != TILE or columns != TILE:
        raise ValueError("unsupported placement")
    heads = width // HEAD_DIM
    slots = 2 if n_h == 2 else 3
    dma = pltpu.SemaphoreType.DMA
    out = pl.pallas_call(
        functools.partial(kernel, n_h, n_w),
        out_shape=jax.ShapeDtypeStruct((count, width), jnp.bfloat16),
        in_specs=[
            pl.BlockSpec(memory_space=pltpu.HBM),
            pl.BlockSpec(memory_space=pltpu.HBM),
            pl.BlockSpec(memory_space=pltpu.HBM),
        ],
        out_specs=pl.BlockSpec(memory_space=pltpu.VMEM),
        scratch_shapes=[
            pltpu.SMEM(tile_mask.shape, jnp.int32),
            pltpu.VMEM((3, frames, rows, columns, features), jnp.bfloat16),
            pltpu.VMEM((3 * count, features), jnp.bfloat16),
            pltpu.VMEM((3, width, features), jnp.bfloat16),
            pltpu.VMEM((heads, count // CUBE, slots * 3 * CUBE, HEAD_DIM), jnp.bfloat16),
            pltpu.VMEM((heads, count // CUBE, slots * 3 * CUBE, HEAD_DIM), jnp.bfloat16),
            pltpu.VMEM((heads, count, HEAD_DIM), jnp.bfloat16),
            pltpu.VMEM((count, slots * 3 * count), jnp.bfloat16),
            dma((5,)), dma((2, 2)), dma((2, 2)), dma((3, 2, 2)), dma((3, 2, 2)), dma((3, 2)), dma((3, 2)),
            dma((2,)), dma((2,)), dma((3, 6, n_h - 1)), dma((3, 6, n_h - 1)), dma((2, 3, 2)), dma((2, 3, 2)),
        ],
        compiler_params=pltpu.CompilerParams(
            collective_id=0, has_side_effects=True, vmem_limit_bytes=VMEM_LIMIT
        ),
    )(*(pltpu.with_memory_space_constraint(a, pltpu.HBM) for a in (tokens, qkv_weight, tile_mask)))
    return out.reshape(clips, frames, rows, columns, width)


def solution(mesh):
    in_specs = (
        P("frame", None, "height", "width", None),
        P(None, ("frame", "height"), None),
        P("frame", None, None, None),
    )
    out_specs = P("frame", None, "height", "width", None)
    body = functools.partial(
        per_device, mesh.shape["frame"], mesh.shape["height"], mesh.shape["width"]
    )
    return jax.shard_map(body, mesh=mesh, in_specs=in_specs, out_specs=out_specs, check_vma=False)
```
